128 devices in a mesh: row: 8 (over y_hi, z), col: 16 (over y_lo, x, core).
Axes of the slice: x: 4, y: 4 (y_hi: 2, y_lo: 2; y = y_hi * 2 + y_lo), z: 4, core: 2. Of those that a mesh axis runs over, the one named last changes fastest.
Arguments:
- tokens: bfloat16 [256, 256, 512], P('row', 'col'), may hold values from -6 to 6
- norm_gains: float32 [4, 512], replicated, may hold values from 0.1 to 1.9
- qkv_weight: bfloat16 [2, 512, 1536], replicated, may hold values from -1 to 1
- rel_bias: float32 [2, 16, 13, 13], replicated, may hold values from -4 to 4
- proj_weight: bfloat16 [2, 512, 512], replicated, may hold values from -0.5 to 0.5
- up_weight: bfloat16 [2, 512, 2048], replicated, may hold values from -0.25 to 0.25
- down_weight: bfloat16 [2, 2048, 512], replicated, may hold values from -0.125 to 0.125
Outputs:
- features: bfloat16 [256, 256, 512], P('row', 'col')
The draws below stay inside these ranges and needn't reach their ends.
All inputs are finite; a program needn't handle non-finite values.
Results may differ from the reference program's by a relative error of at most 0.014.
Values may be sent and summed in bfloat16 or wider, within the bound.
No kernel may reach another device: no remote copies, remote signals or barrier semaphores. Data moves between devices by JAX's collectives and lax.ppermute only.
A program may use at most 320 MiB of HBM per device.

```python
import math
import jax
import jax.numpy as jnp
from jax import lax

D = 512
HEADS = 16
FF = 2048
DILATION = 16
ROWS = 256
COLS = 256


def draw_qkv_weight(key, part):
    base_draw = jnp.clip(jax.random.normal(key, (2, D, 3 * D), jnp.float32), -4.0, 4.0) * D ** (-0.5)
    return jnp.clip(base_draw, -1.0, 1.0).astype(jnp.bfloat16)


def block_levels(rng, shape, split, low, top_value):
    level = 1.0
    for position, parts in split:
        heights = jax.random.uniform(jax.random.fold_in(jax.random.fold_in(rng, 6), position), (parts,), jnp.float32, low / len(split), top_value / len(split))
        level = level * jnp.repeat(jnp.exp(heights), shape[position] // parts).reshape((-1,) + (1,) * (len(shape) - 1 - position))
    return level


def noise(stream_key, dims, spread, bound, cuts=(), kind=jnp.bfloat16):
    gain = block_levels(stream_key, dims, cuts, -0.22, 0.18) if cuts else 1.0
    array = jax.random.normal(stream_key, dims, jnp.float32) * spread * gain
    return jnp.minimum(jnp.maximum(array, -bound), bound).astype(kind)


def setup_inputs(seed: int = 0) -> dict:
    splits = jax.random.split(jax.random.key(seed), 8)
    return {
        "tokens": noise(splits[0], (ROWS, COLS, D), 1.0, 6.0, ((0, 8), (1, 16))),
        "norm_gains": jnp.clip(1.0 + 0.18 * jax.random.normal(splits[1], (4, D), jnp.float32), 0.1, 1.9),
        "qkv_weight": draw_qkv_weight(jax.random.fold_in(splits[7], 71), 0),
        "rel_bias": noise(splits[3], (2, HEADS, 13, 13), 1.0, 4.0, (), jnp.float32),
        "proj_weight": noise(splits[4], (2, D, D), (D // 4) ** -0.5, 0.5),
        "up_weight": noise(splits[5], (2, D, FF), D ** -0.5, 0.25),
        "down_weight": noise(splits[6], (2, FF, D), FF ** -0.5, 0.125),
    }


def window_starts(positions, extent):
    return jnp.clip(positions - 3, 0, extent - 7)

def layer_norm(rows_in, norm_gain):
    values_f = rows_in.astype(jnp.float32)
    mean_value = lax.optimization_barrier(jnp.mean(values_f, axis=-1, keepdims=True))
    centred = values_f - mean_value
    variance = lax.optimization_barrier(jnp.mean(centred * centred, axis=-1, keepdims=True))
    return (centred * lax.rsqrt(variance + 1e-05) * norm_gain).astype(jnp.bfloat16)

def window_attend(queries, key_block, value_block, row_start, col_start, row_shift, col_shift, rel_table):
    query_rows, query_cols, group_count, feature_width = queries.shape
    head_count = rel_table.shape[0]
    head_size = feature_width // head_count
    split_query = queries.reshape(query_rows, query_cols, group_count, head_count, head_size).astype(jnp.float32)
    offsets = jnp.arange(7, dtype=jnp.int32)
    classes = jnp.arange(13, dtype=jnp.int32)
    col_index = col_start[None, :] + offsets[:, None]
    col_hot = ((col_shift[None, :] + offsets[:, None] + 6)[:, :, None] == classes).astype(jnp.float32)
    scaling = head_size ** (-0.5)
    score_list = []
    for offset in range(7):
        window = jnp.take(jnp.take(key_block, row_start + offset, axis=0), col_index, axis=1)
        window = window.reshape(query_rows, 7, query_cols, group_count, head_count, head_size).astype(jnp.float32)
        partial_score = jnp.einsum('icbnd,ixcbnd->ixcbn', split_query, window)
        row_hot = ((row_shift + offset + 6)[:, None] == classes).astype(jnp.float32)
        bias_term = jnp.einsum('iy,xcz,nyz->ixcn', row_hot, col_hot, rel_table, precision=lax.Precision.HIGHEST)
        score_list.append(partial_score * scaling + bias_term[:, :, :, None, :])
    scores = jnp.stack(score_list)
    row_max = lax.optimization_barrier(jnp.max(scores, axis=(0, 2), keepdims=True))
    exponent = jnp.exp(scores - row_max)
    weights = (exponent / lax.optimization_barrier(jnp.sum(exponent, axis=(0, 2), keepdims=True))).astype(jnp.bfloat16)
    running = jnp.zeros((query_rows, query_cols, group_count, head_count, head_size), jnp.float32)
    for offset in range(7):
        window = jnp.take(jnp.take(value_block, row_start + offset, axis=0), col_index, axis=1)
        window = window.reshape(query_rows, 7, query_cols, group_count, head_count, head_size).astype(jnp.float32)
        running = running + jnp.einsum('ixcbn,ixcbnd->icbnd', weights[offset].astype(jnp.float32), window)
    return running.reshape(query_rows, query_cols, group_count, feature_width).astype(jnp.bfloat16)

def row_blocks(function, arrays):
    count = arrays[0].shape[0]
    block = math.gcd(count, 4096)
    blocks = tuple((member.reshape(count // block, block, member.shape[1]) for member in arrays))
    result = lax.map(lambda pieces: function(*pieces), blocks)
    return result.reshape(count, result.shape[-1])

def project_inputs(rows_in, norm_gain, weight):
    return jnp.dot(layer_norm(rows_in, norm_gain), weight, preferred_element_type=jnp.float32).astype(jnp.bfloat16)

def finish_layer(attended, stream, norm_gain, proj, up_proj, down_proj):
    mixed = (jnp.dot(attended, proj, preferred_element_type=jnp.float32) + stream.astype(jnp.float32)).astype(jnp.bfloat16)
    normed = layer_norm(mixed, norm_gain)
    hidden = jax.nn.gelu(jnp.dot(normed, up_proj, preferred_element_type=jnp.float32), approximate=True).astype(jnp.bfloat16)
    return (jnp.dot(hidden, down_proj, preferred_element_type=jnp.float32) + mixed.astype(jnp.float32)).astype(jnp.bfloat16)

def reference(tokens, norm_gains, qkv_weight, rel_bias, proj_weight, up_weight, down_weight):
    map_rows, map_cols, feature_width = tokens.shape
    stream_rows = tokens.reshape(-1, feature_width)
    packed = row_blocks(lambda row_part: project_inputs(row_part, norm_gains[0], qkv_weight[0]), (stream_rows,))
    packed = packed.reshape(map_rows, map_cols, 1, 3 * feature_width)
    queries = packed[..., :feature_width]
    key_block = packed[..., feature_width:2 * feature_width]
    value_block = packed[..., 2 * feature_width:]
    row_begin = window_starts(jnp.arange(map_rows, dtype=jnp.int32), map_rows)
    col_places = jnp.arange(map_cols, dtype=jnp.int32)
    col_begin = window_starts(col_places, map_cols)

    def attend_block(block_index):
        first_row = block_index * 16
        part_query = lax.dynamic_slice_in_dim(queries, first_row, 16, 0)
        part_begin = lax.dynamic_slice_in_dim(row_begin, first_row, 16, 0)
        part_shift = part_begin - (first_row + jnp.arange(16, dtype=jnp.int32))
        return window_attend(part_query, key_block, value_block, part_begin, col_begin, part_shift, col_begin - col_places, rel_bias[0])
    attended = lax.map(attend_block, jnp.arange(map_rows // 16, dtype=jnp.int32)).reshape(-1, feature_width)
    stream_rows = row_blocks(lambda att_part, row_part: finish_layer(att_part, row_part, norm_gains[1], proj_weight[0], up_weight[0], down_weight[0]), (attended, stream_rows))
    group_rows = map_rows // DILATION
    group_cols = map_cols // DILATION
    grouped = stream_rows.reshape(group_rows, DILATION, group_cols, DILATION, feature_width).transpose(1, 3, 0, 2, 4)
    grouped_rows = grouped.reshape(-1, feature_width)
    packed_two = row_blocks(lambda row_part: project_inputs(row_part, norm_gains[2], qkv_weight[1]), (grouped_rows,))
    packed_two = packed_two.reshape(DILATION * DILATION // 16, 16, group_rows, group_cols, 3 * feature_width)
    grow_places = jnp.arange(group_rows, dtype=jnp.int32)
    gcol_places = jnp.arange(group_cols, dtype=jnp.int32)
    grow_begin = window_starts(grow_places, group_rows)
    gcol_begin = window_starts(gcol_places, group_cols)

    def attend_groups(group_part):
        placed = group_part.transpose(1, 2, 0, 3)
        result = window_attend(placed[..., :feature_width], placed[..., feature_width:2 * feature_width], placed[..., 2 * feature_width:], grow_begin, gcol_begin, grow_begin - grow_places, gcol_begin - gcol_places, rel_bias[1])
        return result.transpose(2, 0, 1, 3)
    attended_two = lax.map(attend_groups, packed_two).reshape(-1, feature_width)
    final_rows = row_blocks(lambda att_part, row_part: finish_layer(att_part, row_part, norm_gains[3], proj_weight[1], up_weight[1], down_weight[1]), (attended_two, grouped_rows))
    return final_rows.reshape(DILATION, DILATION, group_rows, group_cols, feature_width).transpose(2, 0, 3, 1, 4).reshape(map_rows, map_cols, feature_width)
```

```python
import jax
import jax.numpy as jnp
from jax import lax
from jax.experimental import pallas as pl
from jax.experimental.pallas import tpu as pltpu
from jax.sharding import PartitionSpec as P

D = 512
HEADS = 16
FF = 2048
TR = 32
TC = 16
MAP = 256
LOG2E = 1.4426950408889634
QSCALE = LOG2E * 32.0 ** -0.5
NEG = -1e30
F32 = jnp.float32
BF16 = jnp.bfloat16
VMEM_LIMIT = 56 * 1024 * 1024


def iota(shape, dim):
    return lax.broadcasted_iota(jnp.int32, shape, dim)


def layer_norm(rows, gain):
    x = rows.astype(F32)
    centred = x - jnp.mean(x, axis=-1, keepdims=True)
    variance = jnp.mean(centred * centred, axis=-1, keepdims=True)
    return (centred * lax.rsqrt(variance + 1e-5) * gain).astype(BF16)


def dot(a, b):
    return jnp.dot(a, b, preferred_element_type=F32)


def dot_t(a, b):
    return lax.dot_general(a, b, (((1,), (1,)), ((), ())), preferred_element_type=F32)


def gelu(z):
    inner = 0.7978845608028654 * (z + 0.044715 * (z * z * z))
    return 0.5 * z * (1.0 + jnp.tanh(inner))


def head_masks(count):
    lane = iota((count, 128), 1) // 32
    return [lane == h for h in range(4)]


def attend_unit(q, k, v_ones, bias):
    n = q.shape[0]
    masks = head_masks(n)
    zero = jnp.zeros_like(q)
    stacked = jnp.concatenate([jnp.where(m, q, zero) for m in masks], axis=0)
    scores = dot_t(stacked, k) + bias
    top = jnp.max(scores, axis=-1, keepdims=True)
    probs = jnp.exp2(scores - top).astype(BF16)
    both = dot(probs, v_ones)
    out = both[:n]
    for h in range(1, 4):
        part = both[h * n : (h + 1) * n]
        wide = jnp.concatenate([masks[h], masks[h]], axis=1)
        out = jnp.where(wide, part, out)
    return (out[:, :128] / out[:, 128:]).astype(BF16)


def finish_rows(attended, stream, gain, wp, wu, wd):
    mixed = (dot(attended, wp) + stream.astype(F32)).astype(BF16)
    normed = layer_norm(mixed, gain)
    acc = mixed.astype(F32)
    for c in range(4):
        hidden = gelu(dot(normed, wu[:, c * 512 : (c + 1) * 512])).astype(BF16)
        acc = acc + dot(hidden, wd[c * 512 : (c + 1) * 512, :])
    return acc.astype(BF16)


def query_kernel(x_ref, gains_ref, w_ref, q_ref):
    q_ref[...] = (dot(layer_norm(x_ref[...], gains_ref[0:1, :]), w_ref[0]) * QSCALE).astype(BF16)


def query_call(x, gains, qkv_weight):
    return pl.pallas_call(
        query_kernel,
        grid=(1,),
        in_specs=[
            pl.BlockSpec((512, 512), lambda i: (0, 0)),
            pl.BlockSpec((4, 512), lambda i: (0, 0)),
            pl.BlockSpec((1, 512, 512), lambda i: (0, 0, 0)),
        ],
        out_specs=pl.BlockSpec((512, 512), lambda i: (0, 0)),
        out_shape=jax.ShapeDtypeStruct((512, 512), BF16),
        compiler_params=pltpu.CompilerParams(vmem_limit_bytes=VMEM_LIMIT),
        cost_estimate=pl.CostEstimate(flops=2 * 512 ** 3, transcendentals=0, bytes_accessed=3 * 512 * 1024),
        name="query",
    )(x, gains, qkv_weight)


def spread(table, n):
    base = jnp.broadcast_to(table[n : n + 1, :], (16, table.shape[1]))
    return pltpu.roll(base, 0, 1, stride=1, stride_axis=0)


def local_bias_kernel(place_ref, table_ref, bias_ref):
    first_row = place_ref[0]
    first_col = place_ref[1]
    row = iota((64, 256), 0)
    lane = iota((64, 256), 1)
    qi = row // 16
    qj = row % 16
    kr = lane // 24
    kc = lane - kr * 24
    col_q = first_col + qj
    col_a = jnp.clip(col_q - 3, 0, MAP - 7)
    col_k = first_col + kc - 3
    col_ok = (col_k >= col_a) & (col_k <= col_a + 6)
    oks = []
    for block in (0, 1, 7):
        row_q = first_row + 4 * block + qi
        row_a = jnp.clip(row_q - 3, 0, MAP - 7)
        row_k = first_row + 4 * block - 3 + kr
        oks.append(col_ok & (row_k >= row_a) & (row_k <= row_a + 6))
    rolled = [pltpu.roll(table_ref[...], 512 - (24 * (3 - i) + 3), 1) for i in range(4)]
    for n in range(HEADS):
        parts = [spread(rolled[i], n)[:, :256] for i in range(4)]
        full = jnp.concatenate(parts, axis=0)
        at = (n % 4) * 64
        for c in range(3):
            bias_ref[c, n // 4, at : at + 64, :] = jnp.where(oks[c], full, NEG)


def local_bias_call(place, table):
    return pl.pallas_call(
        local_bias_kernel,
        in_specs=[pl.BlockSpec(memory_space=pltpu.SMEM), pl.BlockSpec(memory_space=pltpu.VMEM)],
        out_specs=pl.BlockSpec(memory_space=pltpu.VMEM),
        out_shape=jax.ShapeDtypeStruct((3, 4, 256, 256), F32),
        compiler_params=pltpu.CompilerParams(vmem_limit_bytes=VMEM_LIMIT),
        cost_estimate=pl.CostEstimate(flops=4_000_000, transcendentals=0, bytes_accessed=3 * 1024 * 1024),
        name="local_bias",
    )(place, table)


def group_bias_kernel(table_ref, bias_ref):
    row = iota((32, 128), 0)
    lane = iota((32, 128), 1)
    qi = row // 16
    qj = row % 16
    kr = lane // 16
    kc = lane % 16
    col_a = jnp.clip(qj - 3, 0, 9)
    col_ok = (kc >= col_a) & (kc <= col_a + 6)
    classes = ((0, 0), (1, 0), (2, 1), (6, 8), (7, 8))
    rolled = [pltpu.roll(table_ref[...], 256 - (step * 16 + 6), 1) for step in range(8)]
    for n in range(HEADS):
        at = (n % 4) * 32
        for c, (block, start) in enumerate(classes):
            parts = [spread(rolled[start - 2 * block - i + 7], n)[:, :128] for i in range(2)]
            row_a = jnp.clip(2 * block + qi - 3, 0, 9)
            row_k = start + kr
            ok = col_ok & (row_k >= row_a) & (row_k <= row_a + 6)
            bias_ref[c, n // 4, at : at + 32, :] = jnp.where(ok, jnp.concatenate(parts, axis=0), NEG)


def group_bias_call(table):
    return pl.pallas_call(
        group_bias_kernel,
        in_specs=[pl.BlockSpec(memory_space=pltpu.VMEM)],
        out_specs=pl.BlockSpec(memory_space=pltpu.VMEM),
        out_shape=jax.ShapeDtypeStruct((5, 4, 128, 128), F32),
        compiler_params=pltpu.CompilerParams(vmem_limit_bytes=VMEM_LIMIT),
        cost_estimate=pl.CostEstimate(flops=4_000_000, transcendentals=0, bytes_accessed=1_300_000),
        name="group_bias",
    )(table)


def local_kernel(
    xpad_ref, x_ref, q_ref, gains_ref, bias_hbm, wqkv_hbm, wp_hbm, wu_hbm, wd_hbm, out_ref,
    bias, wkv, wp, wu, wd, k_s, v_s, a_s, sems,
):
    copies = [
        pltpu.make_async_copy(wqkv_hbm.at[0, :, pl.ds(512, 1024)], wkv, sems.at[0]),
        pltpu.make_async_copy(bias_hbm, bias, sems.at[1]),
        pltpu.make_async_copy(wp_hbm.at[0], wp, sems.at[2]),
        pltpu.make_async_copy(wu_hbm.at[0], wu, sems.at[3]),
        pltpu.make_async_copy(wd_hbm.at[0], wd, sems.at[4]),
    ]
    for c in copies:
        c.start()
    k_s[912:928, :] = jnp.zeros((16, 512), BF16)
    v_s[...] = jnp.ones((928, 1024), BF16)
    for g in range(4):
        v_s[912:928, g * 256 : g * 256 + 128] = jnp.zeros((16, 128), BF16)
    copies[0].wait()
    for r in range(3):
        rows = slice(r * 304, (r + 1) * 304)
        normed = layer_norm(xpad_ref[rows, :], gains_ref[0:1, :])
        k_s[rows, :] = dot(normed, wkv[:, :512]).astype(BF16)
        value = dot(normed, wkv[:, 512:]).astype(BF16)
        for g in range(4):
            v_s[rows, g * 256 : g * 256 + 128] = value[:, g * 128 : (g + 1) * 128]
    copies[1].wait()

    def attend(b, carry):
        at_q = pl.multiple_of(b * 64, 64)
        at_k = pl.multiple_of(b * 96, 32)
        kind = jnp.where(b == 0, 0, jnp.where(b == 7, 2, 1))
        for g in range(4):
            lanes = slice(g * 128, (g + 1) * 128)
            a_s[pl.ds(at_q, 64), lanes] = attend_unit(
                q_ref[pl.ds(at_q, 64), lanes],
                k_s[pl.ds(at_k, 256), lanes],
                v_s[pl.ds(at_k, 256), g * 256 : (g + 1) * 256],
                bias[kind, g],
            )
        return carry

    lax.fori_loop(0, 8, attend, 0)
    for c in copies[2:]:
        c.wait()
    for half in range(2):
        rows = slice(half * 256, (half + 1) * 256)
        done = finish_rows(a_s[rows, :], x_ref[rows, :], gains_ref[1:2, :], wp[...], wu, wd)
        for r in range(8):
            for g in range(2):
                at = (2 * r + g) * 16
                lane = (g * 2 + half) * 512
                out_ref[r * 16 : (r + 1) * 16, lane : lane + 512] = done[at : at + 16, :]


def local_call(xpad, x, q, gains, bias, wqkv, wp, wu, wd):
    vmem = pl.BlockSpec(memory_space=pltpu.VMEM)
    hbm = pl.BlockSpec(memory_space=pl.ANY)
    return pl.pallas_call(
        local_kernel,
        in_specs=[vmem] * 4 + [hbm] * 5,
        out_specs=vmem,
        out_shape=jax.ShapeDtypeStruct((128, 2048), BF16),
        scratch_shapes=[
            pltpu.VMEM((3, 4, 256, 256), F32),
            pltpu.VMEM((512, 1024), BF16),
            pltpu.VMEM((512, 512), BF16),
            pltpu.VMEM((512, 2048), BF16),
            pltpu.VMEM((2048, 512), BF16),
            pltpu.VMEM((928, 512), BF16),
            pltpu.VMEM((928, 1024), BF16),
            pltpu.VMEM((512, 512), BF16),
            pltpu.SemaphoreType.DMA((5,)),
        ],
        compiler_params=pltpu.CompilerParams(vmem_limit_bytes=VMEM_LIMIT),
        cost_estimate=pl.CostEstimate(flops=8_000_000_000, transcendentals=3_000_000, bytes_accessed=12_000_000),
        name="local_layer",
    )(xpad, x, q, gains, bias, wqkv, wp, wu, wd)


def group_kernel(
    in_ref, gains_ref, bias_hbm, wqkv_hbm, wp_hbm, wu_hbm, wd_hbm, out_ref,
    bias, wqkv, wp, wu, wd, x_s, q_s, k_s, v_s, a_s, sems,
):
    copies = [
        pltpu.make_async_copy(wqkv_hbm.at[1], wqkv, sems.at[0]),
        pltpu.make_async_copy(bias_hbm, bias, sems.at[1]),
        pltpu.make_async_copy(wp_hbm.at[1], wp, sems.at[2]),
        pltpu.make_async_copy(wu_hbm.at[1], wu, sems.at[3]),
        pltpu.make_async_copy(wd_hbm.at[1], wd, sems.at[4]),
    ]
    for c in copies:
        c.start()
    for g in range(2):
        for p in range(16):
            r, half = p // 2, p % 2
            lane = (g * 2 + half) * 512
            at = g * 256 + p * 16
            x_s[at : at + 16, :] = in_ref[r * 16 : (r + 1) * 16, lane : lane + 512]
    v_s[...] = jnp.ones((512, 1024), BF16)
    copies[0].wait()
    for g in range(2):
        rows = slice(g * 256, (g + 1) * 256)
        normed = layer_norm(x_s[rows, :], gains_ref[2:3, :])
        q_s[rows, :] = (dot(normed, wqkv[:, :512]) * QSCALE).astype(BF16)
        k_s[rows, :] = dot(normed, wqkv[:, 512:1024]).astype(BF16)
        value = dot(normed, wqkv[:, 1024:]).astype(BF16)
        for h in range(4):
            v_s[rows, h * 256 : h * 256 + 128] = value[:, h * 128 : (h + 1) * 128]
    copies[1].wait()

    def attend(b, carry):
        start = jnp.clip(2 * b - 3, 0, 8)
        kind = jnp.where(b < 2, b, jnp.where(b < 6, 2, b - 3))
        for g in range(2):
            at_q = pl.multiple_of(g * 256 + b * 32, 32)
            at_k = pl.multiple_of(g * 256 + start * 16, 16)
            for h in range(4):
                lanes = slice(h * 128, (h + 1) * 128)
                a_s[pl.ds(at_q, 32), lanes] = attend_unit(
                    q_s[pl.ds(at_q, 32), lanes],
                    k_s[pl.ds(at_k, 128), lanes],
                    v_s[pl.ds(at_k, 128), h * 256 : (h + 1) * 256],
                    bias[kind, h],
                )
        return carry

    lax.fori_loop(0, 8, attend, 0)
    for c in copies[2:]:
        c.wait()
    for g in range(2):
        rows = slice(g * 256, (g + 1) * 256)
        done = finish_rows(a_s[rows, :], x_s[rows, :], gains_ref[3:4, :], wp[...], wu, wd)
        for p in range(16):
            r, half = p // 2, p % 2
            lane = (g * 2 + half) * 512
            out_ref[r * 16 : (r + 1) * 16, lane : lane + 512] = done[p * 16 : (p + 1) * 16, :]


def group_call(rows, gains, bias, wqkv, wp, wu, wd):
    vmem = pl.BlockSpec(memory_space=pltpu.VMEM)
    hbm = pl.BlockSpec(memory_space=pl.ANY)
    return pl.pallas_call(
        group_kernel,
        in_specs=[vmem] * 2 + [hbm] * 5,
        out_specs=vmem,
        out_shape=jax.ShapeDtypeStruct((128, 2048), BF16),
        scratch_shapes=[
            pltpu.VMEM((5, 4, 128, 128), F32),
            pltpu.VMEM((512, 1536), BF16),
            pltpu.VMEM((512, 512), BF16),
            pltpu.VMEM((512, 2048), BF16),
            pltpu.VMEM((2048, 512), BF16),
            pltpu.VMEM((512, 512), BF16),
            pltpu.VMEM((512, 512), BF16),
            pltpu.VMEM((512, 512), BF16),
            pltpu.VMEM((512, 1024), BF16),
            pltpu.VMEM((512, 512), BF16),
            pltpu.SemaphoreType.DMA((5,)),
        ],
        compiler_params=pltpu.CompilerParams(vmem_limit_bytes=VMEM_LIMIT),
        cost_estimate=pl.CostEstimate(flops=7_000_000_000, transcendentals=3_000_000, bytes_accessed=10_000_000),
        name="group_layer",
    )(rows, gains, bias, wqkv, wp, wu, wd)


def place_kernel(in_ref, out_ref):
    for r in range(8):
        for g in range(2):
            for half in range(2):
                lane = (g * 2 + half) * 512
                out_ref[half * 16 + 2 * r + g] = in_ref[r * 16 : (r + 1) * 16, lane : lane + 512]


def place_call(rows):
    return pl.pallas_call(
        place_kernel,
        in_specs=[pl.BlockSpec(memory_space=pltpu.VMEM)],
        out_specs=pl.BlockSpec(memory_space=pltpu.VMEM),
        out_shape=jax.ShapeDtypeStruct((TR, TC, D), BF16),
        compiler_params=pltpu.CompilerParams(vmem_limit_bytes=VMEM_LIMIT),
        name="place",
    )(rows)


def edges(cells, axis, dim):
    count = lax.axis_size(axis)
    ends = count - 1
    size = cells.shape[dim]
    head = lax.slice_in_dim(cells, 0, 3, axis=dim)
    tail = lax.slice_in_dim(cells, size - 3, size, axis=dim)
    before = lax.ppermute(tail, axis, [(i, i + 1) for i in range(ends)])
    after = lax.ppermute(head, axis, [(i + 1, i) for i in range(ends)])
    return before, after


def exchange(rows):
    shaped = rows.reshape(128, 16, 128)
    return lax.all_to_all(shaped, ("row", "col"), 0, 0, tiled=True).reshape(128, 2048)


def body(tokens, norm_gains, qkv_weight, rel_bias, proj_weight, up_weight, down_weight):
    x = tokens.reshape(TR * TC, D)
    top, bottom = edges(tokens, "row", 0)
    tall = jnp.concatenate([top, tokens, bottom], axis=0)
    left, right = edges(tall, "col", 1)
    xpad = jnp.concatenate([left, tall, right, jnp.zeros((TR + 6, 2, D), BF16)], axis=1)
    xpad = xpad.reshape((TR + 6) * 24, D)

    table = rel_bias * LOG2E
    local_table = jnp.pad(table[0], ((0, 0), (0, 0), (0, 11))).reshape(HEADS, 312)
    local_table = jnp.pad(local_table, ((0, 0), (0, 200)))
    group_table = jnp.pad(table[1], ((0, 0), (1, 2), (0, 3))).reshape(HEADS, 256)
    place = jnp.stack([lax.axis_index("row") * TR, lax.axis_index("col") * TC]).astype(jnp.int32)

    q = query_call(x, norm_gains, qkv_weight)
    local_bias = local_bias_call(place, local_table)
    group_bias = group_bias_call(group_table)
    sent = local_call(xpad, x, q, norm_gains, local_bias, qkv_weight, proj_weight, up_weight, down_weight)
    got = exchange(sent)
    back = group_call(got, norm_gains, group_bias, qkv_weight, proj_weight, up_weight, down_weight)
    return place_call(exchange(back))


def solution(mesh):
    placed = (P("row", "col", None), P(), P(), P(), P(), P(), P())
    return jax.shard_map(
        body, mesh=mesh, in_specs=placed, out_specs=P("row", "col", None), check_vma=False
    )
```

```python
import jax
import jax.numpy as jnp
from jax import lax
from jax.experimental import pallas as pl
from jax.experimental.pallas import tpu as pltpu
from jax.sharding import PartitionSpec as P

D = 512
HEADS = 16
FF = 2048
TR = 32
TC = 16
MAP = 256
LOG2E = 1.4426950408889634
QSCALE = LOG2E * 32.0 ** -0.5
NEG = -1e30
F32 = jnp.float32
BF16 = jnp.bfloat16
VMEM_LIMIT = 56 * 1024 * 1024


def iota(shape, dim):
    return lax.broadcasted_iota(jnp.int32, shape, dim)


def layer_norm(rows, gain):
    x = rows.astype(F32)
    centred = x - jnp.mean(x, axis=-1, keepdims=True)
    variance = jnp.mean(centred * centred, axis=-1, keepdims=True)
    return (centred * lax.rsqrt(variance + 1e-5) * gain).astype(BF16)


def dot(a, b):
    return jnp.dot(a, b, preferred_element_type=F32)


def dot_t(a, b):
    return lax.dot_general(a, b, (((1,), (1,)), ((), ())), preferred_element_type=F32)


def gelu(z):
    inner = 0.7978845608028654 * (z + 0.044715 * (z * z * z))
    return 0.5 * z * (1.0 + jnp.tanh(inner))


def head_masks(count):
    lane = iota((count, 128), 1) // 32
    return [lane == h for h in range(4)]


def attend_units(units):
    n = units[0][0].shape[0]
    masks = head_masks(n)
    zero = jnp.zeros((n, 128), BF16)
    scores = []
    for q, k, _, bias in units:
        stacked = jnp.concatenate([jnp.where(m, q, zero) for m in masks], axis=0)
        scores.append(dot_t(stacked, k) + bias)
    tops = [jnp.max(s, axis=-1, keepdims=True) for s in scores]
    probs = [jnp.exp2(s - t).astype(BF16) for s, t in zip(scores, tops)]
    outs = []
    for unit, p in zip(units, probs):
        both = dot(p, unit[2])
        top, low = both[:n, :128], both[:n, 128:]
        for h in range(1, 4):
            part = both[h * n : (h + 1) * n]
            top = jnp.where(masks[h], part[:, :128], top)
            low = jnp.where(masks[h], part[:, 128:], low)
        outs.append((top / low).astype(BF16))
    return outs


def finish_rows(attended, stream, gain, wp, wu, wd):
    mixed = (dot(attended, wp) + stream.astype(F32)).astype(BF16)
    normed = layer_norm(mixed, gain)
    acc = mixed.astype(F32)
    for c in range(4):
        hidden = gelu(dot(normed, wu[:, c * 512 : (c + 1) * 512])).astype(BF16)
        acc = acc + dot(hidden, wd[c * 512 : (c + 1) * 512, :])
    return acc.astype(BF16)


def query_kernel(x_ref, gains_ref, w_ref, q_ref):
    q_ref[...] = (dot(layer_norm(x_ref[...], gains_ref[0:1, :]), w_ref[0]) * QSCALE).astype(BF16)


def query_call(x, gains, qkv_weight):
    return pl.pallas_call(
        query_kernel,
        grid=(1,),
        in_specs=[
            pl.BlockSpec((512, 512), lambda i: (0, 0)),
            pl.BlockSpec((4, 512), lambda i: (0, 0)),
            pl.BlockSpec((1, 512, 512), lambda i: (0, 0, 0)),
        ],
        out_specs=pl.BlockSpec((512, 512), lambda i: (0, 0)),
        out_shape=jax.ShapeDtypeStruct((512, 512), BF16),
        compiler_params=pltpu.CompilerParams(vmem_limit_bytes=VMEM_LIMIT),
        cost_estimate=pl.CostEstimate(flops=2 * 512 ** 3, transcendentals=0, bytes_accessed=3 * 512 * 1024),
        name="query",
    )(x, gains, qkv_weight)


def spread(table, n):
    base = jnp.broadcast_to(table[n : n + 1, :], (16, table.shape[1]))
    return pltpu.roll(base, 0, 1, stride=1, stride_axis=0)


def local_bias_kernel(place_ref, table_ref, bias_ref):
    first_row = place_ref[0]
    first_col = place_ref[1]
    row = iota((64, 256), 0)
    lane = iota((64, 256), 1)
    qi = row // 16
    qj = row % 16
    kr = lane // 24
    kc = lane - kr * 24
    col_q = first_col + qj
    col_a = jnp.clip(col_q - 3, 0, MAP - 7)
    col_k = first_col + kc - 3
    col_ok = (col_k >= col_a) & (col_k <= col_a + 6)
    oks = []
    for block in (0, 1, 7):
        row_q = first_row + 4 * block + qi
        row_a = jnp.clip(row_q - 3, 0, MAP - 7)
        row_k = first_row + 4 * block - 3 + kr
        oks.append(col_ok & (row_k >= row_a) & (row_k <= row_a + 6))
    rolled = [pltpu.roll(table_ref[...], 512 - (24 * (3 - i) + 3), 1) for i in range(4)]
    for n in range(HEADS):
        parts = [spread(rolled[i], n)[:, :256] for i in range(4)]
        full = jnp.concatenate(parts, axis=0)
        at = (n % 4) * 64
        for c in range(3):
            bias_ref[c, n // 4, at : at + 64, :] = jnp.where(oks[c], full, NEG)


def local_bias_call(place, table):
    return pl.pallas_call(
        local_bias_kernel,
        in_specs=[pl.BlockSpec(memory_space=pltpu.SMEM), pl.BlockSpec(memory_space=pltpu.VMEM)],
        out_specs=pl.BlockSpec(memory_space=pltpu.VMEM),
        out_shape=jax.ShapeDtypeStruct((3, 4, 256, 256), F32),
        compiler_params=pltpu.CompilerParams(vmem_limit_bytes=VMEM_LIMIT),
        cost_estimate=pl.CostEstimate(flops=4_000_000, transcendentals=0, bytes_accessed=3 * 1024 * 1024),
        name="local_bias",
    )(place, table)


def group_bias_kernel(table_ref, bias_ref):
    row = iota((32, 128), 0)
    lane = iota((32, 128), 1)
    qi = row // 16
    qj = row % 16
    kr = lane // 16
    kc = lane % 16
    col_a = jnp.clip(qj - 3, 0, 9)
    col_ok = (kc >= col_a) & (kc <= col_a + 6)
    classes = ((0, 0), (1, 0), (2, 1), (6, 8), (7, 8))
    rolled = [pltpu.roll(table_ref[...], 256 - (step * 16 + 6), 1) for step in range(8)]
    for n in range(HEADS):
        at = (n % 4) * 32
        for c, (block, start) in enumerate(classes):
            parts = [spread(rolled[start - 2 * block - i + 7], n)[:, :128] for i in range(2)]
            row_a = jnp.clip(2 * block + qi - 3, 0, 9)
            row_k = start + kr
            ok = col_ok & (row_k >= row_a) & (row_k <= row_a + 6)
            bias_ref[c, n // 4, at : at + 32, :] = jnp.where(ok, jnp.concatenate(parts, axis=0), NEG)


def group_bias_call(table):
    return pl.pallas_call(
        group_bias_kernel,
        in_specs=[pl.BlockSpec(memory_space=pltpu.VMEM)],
        out_specs=pl.BlockSpec(memory_space=pltpu.VMEM),
        out_shape=jax.ShapeDtypeStruct((5, 4, 128, 128), F32),
        compiler_params=pltpu.CompilerParams(vmem_limit_bytes=VMEM_LIMIT),
        cost_estimate=pl.CostEstimate(flops=4_000_000, transcendentals=0, bytes_accessed=1_300_000),
        name="group_bias",
    )(table)


def local_kernel(
    xpad_ref, x_ref, q_ref, gains_ref, bias_hbm, wqkv_hbm, wp_hbm, wu_hbm, wd_hbm, out_ref,
    bias, wkv, wp, wu, wd, k_s, v_s, a_s, sems,
):
    copies = [
        pltpu.make_async_copy(wqkv_hbm.at[0, :, pl.ds(512, 1024)], wkv, sems.at[0]),
        pltpu.make_async_copy(bias_hbm, bias, sems.at[1]),
        pltpu.make_async_copy(wp_hbm.at[0], wp, sems.at[2]),
        pltpu.make_async_copy(wu_hbm.at[0], wu, sems.at[3]),
        pltpu.make_async_copy(wd_hbm.at[0], wd, sems.at[4]),
    ]
    for c in copies:
        c.start()
    k_s[912:928, :] = jnp.zeros((16, 512), BF16)
    v_s[...] = jnp.ones((928, 1024), BF16)
    for g in range(4):
        v_s[912:928, g * 256 : g * 256 + 128] = jnp.zeros((16, 128), BF16)
    copies[0].wait()
    for r in range(3):
        rows = slice(r * 304, (r + 1) * 304)
        normed = layer_norm(xpad_ref[rows, :], gains_ref[0:1, :])
        k_s[rows, :] = dot(normed, wkv[:, :512]).astype(BF16)
        value = dot(normed, wkv[:, 512:]).astype(BF16)
        for g in range(4):
            v_s[rows, g * 256 : g * 256 + 128] = value[:, g * 128 : (g + 1) * 128]
    copies[1].wait()

    def attend(b, carry):
        at_q = b * 64
        at_k = b * 96
        kind = 0 if b == 0 else 2 if b == 7 else 1
        outs = attend_units(
            [
                (
                    q_ref[pl.ds(at_q, 64), g * 128 : (g + 1) * 128],
                    k_s[pl.ds(at_k, 256), g * 128 : (g + 1) * 128],
                    v_s[pl.ds(at_k, 256), g * 256 : (g + 1) * 256],
                    bias[kind, g],
                )
                for g in range(4)
            ]
        )
        for g in range(4):
            a_s[pl.ds(at_q, 64), g * 128 : (g + 1) * 128] = outs[g]
        return carry

    for b in range(8):
        attend(b, 0)
    for c in copies[2:]:
        c.wait()
    for half in range(2):
        rows = slice(half * 256, (half + 1) * 256)
        done = finish_rows(a_s[rows, :], x_ref[rows, :], gains_ref[1:2, :], wp[...], wu, wd)
        for r in range(8):
            for g in range(2):
                at = (2 * r + g) * 16
                lane = (g * 2 + half) * 512
                out_ref[r * 16 : (r + 1) * 16, lane : lane + 512] = done[at : at + 16, :]


def local_call(xpad, x, q, gains, bias, wqkv, wp, wu, wd):
    vmem = pl.BlockSpec(memory_space=pltpu.VMEM)
    hbm = pl.BlockSpec(memory_space=pl.ANY)
    return pl.pallas_call(
        local_kernel,
        in_specs=[vmem] * 4 + [hbm] * 5,
        out_specs=vmem,
        out_shape=jax.ShapeDtypeStruct((128, 2048), BF16),
        scratch_shapes=[
            pltpu.VMEM((3, 4, 256, 256), F32),
            pltpu.VMEM((512, 1024), BF16),
            pltpu.VMEM((512, 512), BF16),
            pltpu.VMEM((512, 2048), BF16),
            pltpu.VMEM((2048, 512), BF16),
            pltpu.VMEM((928, 512), BF16),
            pltpu.VMEM((928, 1024), BF16),
            pltpu.VMEM((512, 512), BF16),
            pltpu.SemaphoreType.DMA((5,)),
        ],
        compiler_params=pltpu.CompilerParams(vmem_limit_bytes=VMEM_LIMIT),
        cost_estimate=pl.CostEstimate(flops=8_000_000_000, transcendentals=3_000_000, bytes_accessed=12_000_000),
        name="local_layer",
    )(xpad, x, q, gains, bias, wqkv, wp, wu, wd)


def group_kernel(
    in_ref, gains_ref, bias_hbm, wqkv_hbm, wp_hbm, wu_hbm, wd_hbm, out_ref,
    bias, wqkv, wp, wu, wd, x_s, q_s, k_s, v_s, a_s, sems,
):
    copies = [
        pltpu.make_async_copy(wqkv_hbm.at[1], wqkv, sems.at[0]),
        pltpu.make_async_copy(bias_hbm, bias, sems.at[1]),
        pltpu.make_async_copy(wp_hbm.at[1], wp, sems.at[2]),
        pltpu.make_async_copy(wu_hbm.at[1], wu, sems.at[3]),
        pltpu.make_async_copy(wd_hbm.at[1], wd, sems.at[4]),
    ]
    for c in copies:
        c.start()
    for g in range(2):
        for p in range(16):
            r, half = p // 2, p % 2
            lane = (g * 2 + half) * 512
            at = g * 256 + p * 16
            x_s[at : at + 16, :] = in_ref[r * 16 : (r + 1) * 16, lane : lane + 512]
    v_s[...] = jnp.ones((512, 1024), BF16)
    copies[0].wait()
    for g in range(2):
        rows = slice(g * 256, (g + 1) * 256)
        normed = layer_norm(x_s[rows, :], gains_ref[2:3, :])
        q_s[rows, :] = (dot(normed, wqkv[:, :512]) * QSCALE).astype(BF16)
        k_s[rows, :] = dot(normed, wqkv[:, 512:1024]).astype(BF16)
        value = dot(normed, wqkv[:, 1024:]).astype(BF16)
        for h in range(4):
            v_s[rows, h * 256 : h * 256 + 128] = value[:, h * 128 : (h + 1) * 128]
    copies[1].wait()

    def attend(b, carry):
        start = min(max(2 * b - 3, 0), 8)
        kind = b if b < 2 else 2 if b < 6 else b - 3
        units = []
        for g in range(2):
            at_q = g * 256 + b * 32
            at_k = g * 256 + start * 16
            for h in range(4):
                units.append(
                    (
                        q_s[pl.ds(at_q, 32), h * 128 : (h + 1) * 128],
                        k_s[pl.ds(at_k, 128), h * 128 : (h + 1) * 128],
                        v_s[pl.ds(at_k, 128), h * 256 : (h + 1) * 256],
                        bias[kind, h],
                    )
                )
        outs = attend_units(units)
        for g in range(2):
            at_q = g * 256 + b * 32
            for h in range(4):
                a_s[pl.ds(at_q, 32), h * 128 : (h + 1) * 128] = outs[g * 4 + h]
        return carry

    for b in range(8):
        attend(b, 0)
    for c in copies[2:]:
        c.wait()
    for g in range(2):
        rows = slice(g * 256, (g + 1) * 256)
        done = finish_rows(a_s[rows, :], x_s[rows, :], gains_ref[3:4, :], wp[...], wu, wd)
        for p in range(16):
            r, half = p // 2, p % 2
            lane = (g * 2 + half) * 512
            out_ref[r * 16 : (r + 1) * 16, lane : lane + 512] = done[p * 16 : (p + 1) * 16, :]


def group_call(rows, gains, bias, wqkv, wp, wu, wd):
    vmem = pl.BlockSpec(memory_space=pltpu.VMEM)
    hbm = pl.BlockSpec(memory_space=pl.ANY)
    return pl.pallas_call(
        group_kernel,
        in_specs=[vmem] * 2 + [hbm] * 5,
        out_specs=vmem,
        out_shape=jax.ShapeDtypeStruct((128, 2048), BF16),
        scratch_shapes=[
            pltpu.VMEM((5, 4, 128, 128), F32),
            pltpu.VMEM((512, 1536), BF16),
            pltpu.VMEM((512, 512), BF16),
            pltpu.VMEM((512, 2048), BF16),
            pltpu.VMEM((2048, 512), BF16),
            pltpu.VMEM((512, 512), BF16),
            pltpu.VMEM((512, 512), BF16),
            pltpu.VMEM((512, 512), BF16),
            pltpu.VMEM((512, 1024), BF16),
            pltpu.VMEM((512, 512), BF16),
            pltpu.SemaphoreType.DMA((5,)),
        ],
        compiler_params=pltpu.CompilerParams(vmem_limit_bytes=VMEM_LIMIT),
        cost_estimate=pl.CostEstimate(flops=7_000_000_000, transcendentals=3_000_000, bytes_accessed=10_000_000),
        name="group_layer",
    )(rows, gains, bias, wqkv, wp, wu, wd)


def place_kernel(in_ref, out_ref):
    for r in range(8):
        for g in range(2):
            for half in range(2):
                lane = (g * 2 + half) * 512
                out_ref[half * 16 + 2 * r + g] = in_ref[r * 16 : (r + 1) * 16, lane : lane + 512]


def place_call(rows):
    return pl.pallas_call(
        place_kernel,
        in_specs=[pl.BlockSpec(memory_space=pltpu.VMEM)],
        out_specs=pl.BlockSpec(memory_space=pltpu.VMEM),
        out_shape=jax.ShapeDtypeStruct((TR, TC, D), BF16),
        compiler_params=pltpu.CompilerParams(vmem_limit_bytes=VMEM_LIMIT),
        name="place",
    )(rows)


def edges(cells, axis, dim):
    count = lax.axis_size(axis)
    ends = count - 1
    size = cells.shape[dim]
    head = lax.slice_in_dim(cells, 0, 3, axis=dim)
    tail = lax.slice_in_dim(cells, size - 3, size, axis=dim)
    before = lax.ppermute(tail, axis, [(i, i + 1) for i in range(ends)])
    after = lax.ppermute(head, axis, [(i + 1, i) for i in range(ends)])
    return before, after


def exchange(rows):
    shaped = rows.reshape(128, 16, 128)
    return lax.all_to_all(shaped, ("row", "col"), 0, 0, tiled=True).reshape(128, 2048)


def body(tokens, norm_gains, qkv_weight, rel_bias, proj_weight, up_weight, down_weight):
    x = tokens.reshape(TR * TC, D)
    top, bottom = edges(tokens, "row", 0)
    tall = jnp.concatenate([top, tokens, bottom], axis=0)
    left, right = edges(tall, "col", 1)
    xpad = jnp.concatenate([left, tall, right, jnp.zeros((TR + 6, 2, D), BF16)], axis=1)
    xpad = xpad.reshape((TR + 6) * 24, D)

    table = rel_bias * LOG2E
    local_table = jnp.pad(table[0], ((0, 0), (0, 0), (0, 11))).reshape(HEADS, 312)
    local_table = jnp.pad(local_table, ((0, 0), (0, 200)))
    group_table = jnp.pad(table[1], ((0, 0), (1, 2), (0, 3))).reshape(HEADS, 256)
    place = jnp.stack([lax.axis_index("row") * TR, lax.axis_index("col") * TC]).astype(jnp.int32)

    q = query_call(x, norm_gains, qkv_weight)
    local_bias = local_bias_call(place, local_table)
    group_bias = group_bias_call(group_table)
    sent = local_call(xpad, x, q, norm_gains, local_bias, qkv_weight, proj_weight, up_weight, down_weight)
    got = exchange(sent)
    back = group_call(got, norm_gains, group_bias, qkv_weight, proj_weight, up_weight, down_weight)
    return place_call(exchange(back))


def solution(mesh):
    placed = (P("row", "col", None), P(), P(), P(), P(), P(), P())
    return jax.shard_map(
        body, mesh=mesh, in_specs=placed, out_specs=P("row", "col", None), check_vma=False
    )
```

```python
import jax
import jax.numpy as jnp
from jax import lax
from jax.experimental import pallas as pl
from jax.experimental.pallas import tpu as pltpu
from jax.sharding import PartitionSpec as P

D = 512
HEADS = 16
FF = 2048
TR = 32
TC = 16
MAP = 256
LOG2E = 1.4426950408889634
QSCALE = LOG2E * 32.0 ** -0.5
NEG = -1e30
F32 = jnp.float32
BF16 = jnp.bfloat16
BIG = 24 * 1024 * 1024
SMALL = 12 * 1024 * 1024
VM = pl.BlockSpec(memory_space=pltpu.VMEM)
FAR = pl.BlockSpec(memory_space=pl.ANY)


def iota(shape, dim):
    return lax.broadcasted_iota(jnp.int32, shape, dim)


def layer_norm(rows, gain):
    x = rows.astype(F32)
    centred = x - jnp.mean(x, axis=-1, keepdims=True)
    variance = jnp.mean(centred * centred, axis=-1, keepdims=True)
    return (centred * lax.rsqrt(variance + 1e-5) * gain).astype(BF16)


def dot(a, b):
    return jnp.dot(a, b, preferred_element_type=F32)


def dot_t(a, b):
    return lax.dot_general(a, b, (((1,), (1,)), ((), ())), preferred_element_type=F32)


def gelu(z):
    inner = 0.7978845608028654 * (z + 0.044715 * (z * z * z))
    return 0.5 * z * (1.0 + jnp.tanh(inner))


def head_masks(count):
    lane = iota((count, 128), 1) // 32
    return [lane == h for h in range(4)]


def attend_units(units):
    n = units[0][0].shape[0]
    masks = head_masks(n)
    zero = jnp.zeros((n, 128), BF16)
    scores = []
    for q, k, _, bias in units:
        stacked = jnp.concatenate([jnp.where(m, q, zero) for m in masks], axis=0)
        scores.append(dot_t(stacked, k) + bias)
    tops = [jnp.max(s, axis=-1, keepdims=True) for s in scores]
    probs = [jnp.exp2(s - t).astype(BF16) for s, t in zip(scores, tops)]
    outs = []
    for unit, p in zip(units, probs):
        both = dot(p, unit[2])
        top, low = both[:n, :128], both[:n, 128:]
        for h in range(1, 4):
            part = both[h * n : (h + 1) * n]
            top = jnp.where(masks[h], part[:, :128], top)
            low = jnp.where(masks[h], part[:, 128:], low)
        outs.append((top / low).astype(BF16))
    return outs


def finish_rows(attended, stream, gain, wp, wu, wd):
    mixed = (dot(attended, wp[...]) + stream.astype(F32)).astype(BF16)
    normed = layer_norm(mixed, gain)
    acc = mixed.astype(F32)
    for c in range(4):
        hidden = gelu(dot(normed, wu[:, c * 512 : (c + 1) * 512])).astype(BF16)
        acc = acc + dot(hidden, wd[c * 512 : (c + 1) * 512, :])
    return acc


def query_kernel(x_ref, gains_ref, w_ref, q_ref):
    for half in range(2):
        rows = slice(half * 256, (half + 1) * 256)
        normed = layer_norm(x_ref[rows, :], gains_ref[0:1, :])
        q_ref[rows, :] = (dot(normed, w_ref[0, :, :512]) * QSCALE).astype(BF16)


def query_call(x, gains, wqkv):
    return pl.pallas_call(
        query_kernel,
        in_specs=[VM] * 3,
        out_specs=VM,
        out_shape=pltpu.VMEM((512, 512), BF16),
        compiler_params=pltpu.CompilerParams(vmem_limit_bytes=SMALL),
        cost_estimate=pl.CostEstimate(flops=2 * 512 ** 3, transcendentals=0, bytes_accessed=3 * 512 * 1024),
        name="query",
    )(x, gains, wqkv)


def spread(table, n):
    base = jnp.broadcast_to(table[n : n + 1, :], (16, table.shape[1]))
    return pltpu.roll(base, 0, 1, stride=1, stride_axis=0)


def local_bias_kernel(place_ref, table_ref, bias_ref):
    first_row = place_ref[0]
    first_col = place_ref[1]
    row = iota((64, 256), 0)
    lane = iota((64, 256), 1)
    qi = row // 16
    qj = row % 16
    kr = lane // 24
    kc = lane - kr * 24
    col_q = first_col + qj
    col_a = jnp.clip(col_q - 3, 0, MAP - 7)
    col_k = first_col + kc - 3
    col_ok = (col_k >= col_a) & (col_k <= col_a + 6)
    oks = []
    for block in (0, 1, 7):
        row_q = first_row + 4 * block + qi
        row_a = jnp.clip(row_q - 3, 0, MAP - 7)
        row_k = first_row + 4 * block - 3 + kr
        oks.append(col_ok & (row_k >= row_a) & (row_k <= row_a + 6))
    rolled = [pltpu.roll(table_ref[...], 512 - (24 * (3 - i) + 3), 1) for i in range(4)]
    for n in range(HEADS):
        parts = [spread(rolled[i], n)[:, :256] for i in range(4)]
        full = jnp.concatenate(parts, axis=0)
        at = (n % 4) * 64
        for c in range(3):
            bias_ref[c, n // 4, at : at + 64, :] = jnp.where(oks[c], full, NEG)


def local_bias_call(place, table):
    return pl.pallas_call(
        local_bias_kernel,
        in_specs=[pl.BlockSpec(memory_space=pltpu.SMEM), VM],
        out_specs=VM,
        out_shape=pltpu.VMEM((3, 4, 256, 256), F32),
        compiler_params=pltpu.CompilerParams(vmem_limit_bytes=SMALL),
        cost_estimate=pl.CostEstimate(flops=4_000_000, transcendentals=0, bytes_accessed=3 * 1024 * 1024),
        name="local_bias",
    )(place, table)


def group_bias_kernel(table_ref, bias_ref):
    row = iota((32, 128), 0)
    lane = iota((32, 128), 1)
    qi = row // 16
    qj = row % 16
    kr = lane // 16
    kc = lane % 16
    col_a = jnp.clip(qj - 3, 0, 9)
    col_ok = (kc >= col_a) & (kc <= col_a + 6)
    classes = ((0, 0), (1, 0), (2, 1), (6, 8), (7, 8))
    rolled = [pltpu.roll(table_ref[...], 256 - (step * 16 + 6), 1) for step in range(8)]
    for n in range(HEADS):
        at = (n % 4) * 32
        for c, (block, start) in enumerate(classes):
            parts = [spread(rolled[start - 2 * block - i + 7], n)[:, :128] for i in range(2)]
            row_a = jnp.clip(2 * block + qi - 3, 0, 9)
            row_k = start + kr
            ok = col_ok & (row_k >= row_a) & (row_k <= row_a + 6)
            bias_ref[c, n // 4, at : at + 32, :] = jnp.where(ok, jnp.concatenate(parts, axis=0), NEG)


def group_bias_call(table):
    return pl.pallas_call(
        group_bias_kernel,
        in_specs=[VM],
        out_specs=VM,
        out_shape=pltpu.VMEM((5, 4, 128, 128), F32),
        compiler_params=pltpu.CompilerParams(vmem_limit_bytes=SMALL),
        cost_estimate=pl.CostEstimate(flops=4_000_000, transcendentals=0, bytes_accessed=1_300_000),
        name="group_bias",
    )(table)


def fetch_weights(layer, far, near, sems):
    copies = [pltpu.make_async_copy(a.at[layer], b, sems.at[i]) for i, (a, b) in enumerate(zip(far, near))]
    for c in copies:
        c.start()
    return copies


WEIGHT_SCRATCH = [
    pltpu.VMEM((512, 512), BF16),
    pltpu.VMEM((512, 2048), BF16),
    pltpu.VMEM((2048, 512), BF16),
    pltpu.SemaphoreType.DMA((3,)),
]


def send_rows(done, stage, pieces):
    for at, block, slot in pieces:
        for f in range(4):
            stage[pl.ds(block * 256 + slot * 4 + f, 16, stride=16), :] = done[at : at + 16, f * 128 : (f + 1) * 128]


def local_kernel(
    xpad_ref, x_ref, q_ref, gains_ref, bias, wqkv, wp_far, wu_far, wd_far, out_ref,
    k_s, v_s, a_s, stage, wp, wu, wd, sems,
):
    copies = fetch_weights(0, (wp_far, wu_far, wd_far), (wp, wu, wd), sems)
    k_s[912:928, :] = jnp.zeros((16, 512), BF16)
    v_s[...] = jnp.ones((928, 1024), BF16)
    for g in range(4):
        v_s[912:928, g * 256 : g * 256 + 128] = jnp.zeros((16, 128), BF16)
    for r in range(3):
        rows = slice(r * 304, (r + 1) * 304)
        normed = layer_norm(xpad_ref[rows, :], gains_ref[0:1, :])
        k_s[rows, :] = dot(normed, wqkv[0, :, 512:1024]).astype(BF16)
        value = dot(normed, wqkv[0, :, 1024:]).astype(BF16)
        for g in range(4):
            v_s[rows, g * 256 : g * 256 + 128] = value[:, g * 128 : (g + 1) * 128]

    def attend(b, carry):
        at_q = b * 64
        at_k = b * 96
        kind = 0 if b == 0 else 2 if b == 7 else 1
        outs = attend_units(
            [
                (
                    q_ref[pl.ds(at_q, 64), g * 128 : (g + 1) * 128],
                    k_s[pl.ds(at_k, 256), g * 128 : (g + 1) * 128],
                    v_s[pl.ds(at_k, 256), g * 256 : (g + 1) * 256],
                    bias[kind, g],
                )
                for g in range(4)
            ]
        )
        for g in range(4):
            a_s[pl.ds(at_q, 64), g * 128 : (g + 1) * 128] = outs[g]
        return carry

    for b in range(8):
        attend(b, 0)
    for c in copies:
        c.wait()
    for half in range(2):
        rows = slice(half * 256, (half + 1) * 256)
        done = finish_rows(a_s[rows, :], x_ref[rows, :], gains_ref[1:2, :], wp, wu, wd)
        send_rows(done, stage, [((2 * r + g) * 16, r, g * 2 + half) for r in range(8) for g in range(2)])
    out_ref[...] = stage[...].reshape(128, 16, 128).astype(BF16)


def local_call(xpad, x, q, gains, bias, wqkv, wp, wu, wd):
    return pl.pallas_call(
        local_kernel,
        in_specs=[VM] * 6 + [FAR] * 3,
        out_specs=VM,
        out_shape=pltpu.VMEM((128, 16, 128), BF16),
        scratch_shapes=[
            pltpu.VMEM((928, 512), BF16),
            pltpu.VMEM((928, 1024), BF16),
            pltpu.VMEM((512, 512), BF16),
            pltpu.VMEM((2048, 128), F32),
        ]
        + WEIGHT_SCRATCH,
        compiler_params=pltpu.CompilerParams(vmem_limit_bytes=BIG),
        cost_estimate=pl.CostEstimate(flops=8_000_000_000, transcendentals=3_000_000, bytes_accessed=12_000_000),
        name="local_layer",
    )(xpad, x, q, gains, bias, wqkv, wp, wu, wd)


def group_kernel(
    in_ref, gains_ref, bias, wqkv, wp_far, wu_far, wd_far, out_ref,
    x_s, q_s, k_s, v_s, a_s, stage, wp, wu, wd, sems,
):
    copies = fetch_weights(1, (wp_far, wu_far, wd_far), (wp, wu, wd), sems)
    stage[...] = in_ref[...].astype(F32).reshape(2048, 128)
    for g in range(2):
        for p in range(16):
            r, half = p // 2, p % 2
            at = g * 256 + p * 16
            for f in range(4):
                x_s[at : at + 16, f * 128 : (f + 1) * 128] = stage[
                    pl.ds(r * 256 + (g * 2 + half) * 4 + f, 16, stride=16), :
                ]
    v_s[...] = jnp.ones((512, 1024), BF16)
    for g in range(2):
        rows = slice(g * 256, (g + 1) * 256)
        normed = layer_norm(x_s[rows, :], gains_ref[2:3, :])
        q_s[rows, :] = (dot(normed, wqkv[1, :, :512]) * QSCALE).astype(BF16)
        k_s[rows, :] = dot(normed, wqkv[1, :, 512:1024]).astype(BF16)
        value = dot(normed, wqkv[1, :, 1024:]).astype(BF16)
        for h in range(4):
            v_s[rows, h * 256 : h * 256 + 128] = value[:, h * 128 : (h + 1) * 128]

    def attend(b, carry):
        start = min(max(2 * b - 3, 0), 8)
        kind = b if b < 2 else 2 if b < 6 else b - 3
        units = []
        for g in range(2):
            at_q = g * 256 + b * 32
            at_k = g * 256 + start * 16
            for h in range(4):
                units.append(
                    (
                        q_s[pl.ds(at_q, 32), h * 128 : (h + 1) * 128],
                        k_s[pl.ds(at_k, 128), h * 128 : (h + 1) * 128],
                        v_s[pl.ds(at_k, 128), h * 256 : (h + 1) * 256],
                        bias[kind, h],
                    )
                )
        outs = attend_units(units)
        for g in range(2):
            at_q = g * 256 + b * 32
            for h in range(4):
                a_s[pl.ds(at_q, 32), h * 128 : (h + 1) * 128] = outs[g * 4 + h]
        return carry

    for b in range(8):
        attend(b, 0)
    for c in copies:
        c.wait()
    for g in range(2):
        rows = slice(g * 256, (g + 1) * 256)
        done = finish_rows(a_s[rows, :], x_s[rows, :], gains_ref[3:4, :], wp, wu, wd)
        send_rows(done, stage, [(p * 16, p // 2, g * 2 + p % 2) for p in range(16)])
    out_ref[...] = stage[...].reshape(128, 16, 128).astype(BF16)


def group_call(rows, gains, bias, wqkv, wp, wu, wd):
    return pl.pallas_call(
        group_kernel,
        in_specs=[VM] * 4 + [FAR] * 3,
        out_specs=VM,
        out_shape=pltpu.VMEM((128, 16, 128), BF16),
        scratch_shapes=[
            pltpu.VMEM((512, 512), F32),
            pltpu.VMEM((512, 512), BF16),
            pltpu.VMEM((512, 512), BF16),
            pltpu.VMEM((512, 1024), BF16),
            pltpu.VMEM((512, 512), BF16),
            pltpu.VMEM((2048, 128), F32),
        ]
        + WEIGHT_SCRATCH,
        compiler_params=pltpu.CompilerParams(vmem_limit_bytes=BIG),
        cost_estimate=pl.CostEstimate(flops=7_000_000_000, transcendentals=3_000_000, bytes_accessed=10_000_000),
        name="group_layer",
    )(rows, gains, bias, wqkv, wp, wu, wd)


def place_kernel(in_ref, out_ref, stage):
    stage[...] = in_ref[...].astype(F32).reshape(2048, 128)
    for r in range(8):
        for slot in range(4):
            parts = [stage[pl.ds(r * 256 + slot * 4 + f, 16, stride=16), :] for f in range(4)]
            out_ref[slot % 2 * 16 + 2 * r + slot // 2] = jnp.concatenate(parts, axis=1).astype(BF16)


def place_call(rows):
    return pl.pallas_call(
        place_kernel,
        in_specs=[VM],
        out_specs=VM,
        out_shape=jax.ShapeDtypeStruct((TR, TC, D), BF16),
        scratch_shapes=[pltpu.VMEM((2048, 128), F32)],
        compiler_params=pltpu.CompilerParams(vmem_limit_bytes=SMALL),
        name="place",
    )(rows)


def edges(cells, axis, dim):
    count = lax.axis_size(axis)
    ends = count - 1
    size = cells.shape[dim]
    head = lax.slice_in_dim(cells, 0, 3, axis=dim)
    tail = lax.slice_in_dim(cells, size - 3, size, axis=dim)
    before = lax.ppermute(tail, axis, [(i, i + 1) for i in range(ends)])
    after = lax.ppermute(head, axis, [(i + 1, i) for i in range(ends)])
    return before, after


def exchange(rows):
    return lax.all_to_all(rows, ("row", "col"), 0, 0, tiled=True)


def body(tokens, norm_gains, qkv_weight, rel_bias, proj_weight, up_weight, down_weight):
    x = tokens.reshape(TR * TC, D)
    top, bottom = edges(tokens, "row", 0)
    tall = jnp.concatenate([top, tokens, bottom], axis=0)
    left, right = edges(tall, "col", 1)
    xpad = jnp.concatenate([left, tall, right, jnp.zeros((TR + 6, 2, D), BF16)], axis=1)
    xpad = xpad.reshape((TR + 6) * 24, D)

    table = rel_bias * LOG2E
    local_table = jnp.pad(table[0], ((0, 0), (0, 0), (0, 11))).reshape(HEADS, 312)
    local_table = jnp.pad(local_table, ((0, 0), (0, 200)))
    group_table = jnp.pad(table[1], ((0, 0), (1, 2), (0, 3))).reshape(HEADS, 256)
    place = jnp.stack([lax.axis_index("row") * TR, lax.axis_index("col") * TC]).astype(jnp.int32)

    near = lambda a: pltpu.with_memory_space_constraint(a, pltpu.VMEM)
    wqkv, wp, wu, wd = near(qkv_weight), proj_weight, up_weight, down_weight
    x = near(x)
    q = query_call(x, norm_gains, wqkv)
    local_bias = local_bias_call(place, local_table)
    group_bias = group_bias_call(group_table)
    sent = local_call(near(xpad), x, q, norm_gains, local_bias, wqkv, wp, wu, wd)
    got = exchange(sent)
    back = group_call(near(got), norm_gains, group_bias, wqkv, wp, wu, wd)
    return place_call(near(exchange(back)))


def solution(mesh):
    placed = (P("row", "col", None), P(), P(), P(), P(), P(), P())
    return jax.shard_map(
        body, mesh=mesh, in_specs=placed, out_specs=P("row", "col", None), check_vma=False
    )
```

```python
import jax
import jax.numpy as jnp
from jax import lax
from jax.experimental import pallas as pl
from jax.experimental.pallas import tpu as pltpu
from jax.sharding import PartitionSpec as P

D = 512
HEADS = 16
FF = 2048
TR = 32
TC = 16
MAP = 256
LOG2E = 1.4426950408889634
QSCALE = LOG2E * 32.0 ** -0.5
NEG = -1e30
F32 = jnp.float32
BF16 = jnp.bfloat16
BIG = 24 * 1024 * 1024
SMALL = 12 * 1024 * 1024
VM = pl.BlockSpec(memory_space=pltpu.VMEM)
FAR = pl.BlockSpec(memory_space=pltpu.HBM)


def iota(shape, dim):
    return lax.broadcasted_iota(jnp.int32, shape, dim)


def layer_norm(rows, gain):
    x = rows.astype(F32)
    centred = x - jnp.mean(x, axis=-1, keepdims=True)
    variance = jnp.mean(centred * centred, axis=-1, keepdims=True)
    return (centred * lax.rsqrt(variance + 1e-5) * gain).astype(BF16)


def dot(a, b):
    return jnp.dot(a, b, preferred_element_type=F32)


def dot_t(a, b):
    return lax.dot_general(a, b, (((1,), (1,)), ((), ())), preferred_element_type=F32)


def gelu(z):
    inner = 0.7978845608028654 * (z + 0.044715 * (z * z * z))
    return 0.5 * z * (1.0 + jnp.tanh(inner))


def head_masks(count):
    lane = iota((count, 128), 1) // 32
    return [lane == h for h in range(4)]


def attend_units(units):
    n = units[0][0].shape[0]
    masks = head_masks(n)
    zero = jnp.zeros((n, 128), BF16)
    scores = []
    for q, k, _, bias in units:
        stacked = jnp.concatenate([jnp.where(m, q, zero) for m in masks], axis=0)
        scores.append(dot_t(stacked, k) + bias)
    tops = [jnp.max(s, axis=-1, keepdims=True) for s in scores]
    probs = [jnp.exp2(s - t).astype(BF16) for s, t in zip(scores, tops)]
    outs = []
    for unit, p in zip(units, probs):
        both = dot(p, unit[2])
        top, low = both[:n, :128], both[:n, 128:]
        for h in range(1, 4):
            part = both[h * n : (h + 1) * n]
            top = jnp.where(masks[h], part[:, :128], top)
            low = jnp.where(masks[h], part[:, 128:], low)
        outs.append((top / low).astype(BF16))
    return outs


def finish_rows(attended, stream, gain, wp, wu, wd):
    mixed = (dot(attended, wp[...]) + stream.astype(F32)).astype(BF16)
    normed = layer_norm(mixed, gain)
    acc = mixed.astype(F32)
    for c in range(4):
        hidden = gelu(dot(normed, wu[:, c * 512 : (c + 1) * 512])).astype(BF16)
        acc = acc + dot(hidden, wd[c * 512 : (c + 1) * 512, :])
    return acc


def query_kernel(x_ref, gains_ref, w_ref, q_ref):
    for half in range(2):
        rows = slice(half * 256, (half + 1) * 256)
        normed = layer_norm(x_ref[rows, :], gains_ref[0:1, :])
        q_ref[rows, :] = (dot(normed, w_ref[0, :, :512]) * QSCALE).astype(BF16)


def query_call(x, gains, wqkv):
    return pl.pallas_call(
        query_kernel,
        in_specs=[VM] * 3,
        out_specs=VM,
        out_shape=pltpu.VMEM((512, 512), BF16),
        compiler_params=pltpu.CompilerParams(vmem_limit_bytes=SMALL),
        cost_estimate=pl.CostEstimate(flops=2 * 512 ** 3, transcendentals=0, bytes_accessed=3 * 512 * 1024),
        name="query",
    )(x, gains, wqkv)


def spread(table, n):
    base = jnp.broadcast_to(table[n : n + 1, :], (16, table.shape[1]))
    return pltpu.roll(base, 0, 1, stride=1, stride_axis=0)


def local_bias_kernel(place_ref, table_ref, bias_ref):
    first_row = place_ref[0]
    first_col = place_ref[1]
    row = iota((64, 256), 0)
    lane = iota((64, 256), 1)
    qi = row // 16
    qj = row % 16
    kr = lane // 24
    kc = lane - kr * 24
    col_q = first_col + qj
    col_a = jnp.clip(col_q - 3, 0, MAP - 7)
    col_k = first_col + kc - 3
    col_ok = (col_k >= col_a) & (col_k <= col_a + 6)
    oks = []
    for block in (0, 1, 7):
        row_q = first_row + 4 * block + qi
        row_a = jnp.clip(row_q - 3, 0, MAP - 7)
        row_k = first_row + 4 * block - 3 + kr
        oks.append(col_ok & (row_k >= row_a) & (row_k <= row_a + 6))
    rolled = [pltpu.roll(table_ref[...], 512 - (24 * (3 - i) + 3), 1) for i in range(4)]
    for n in range(HEADS):
        parts = [spread(rolled[i], n)[:, :256] for i in range(4)]
        full = jnp.concatenate(parts, axis=0)
        at = (n % 4) * 64
        for c in range(3):
            bias_ref[c, n // 4, at : at + 64, :] = jnp.where(oks[c], full, NEG)


def local_bias_call(place, table):
    return pl.pallas_call(
        local_bias_kernel,
        in_specs=[pl.BlockSpec(memory_space=pltpu.SMEM), VM],
        out_specs=VM,
        out_shape=pltpu.VMEM((3, 4, 256, 256), F32),
        compiler_params=pltpu.CompilerParams(vmem_limit_bytes=SMALL),
        cost_estimate=pl.CostEstimate(flops=4_000_000, transcendentals=0, bytes_accessed=3 * 1024 * 1024),
        name="local_bias",
    )(place, table)


def group_bias_kernel(table_ref, bias_ref):
    row = iota((32, 128), 0)
    lane = iota((32, 128), 1)
    qi = row // 16
    qj = row % 16
    kr = lane // 16
    kc = lane % 16
    col_a = jnp.clip(qj - 3, 0, 9)
    col_ok = (kc >= col_a) & (kc <= col_a + 6)
    classes = ((0, 0), (1, 0), (2, 1), (6, 8), (7, 8))
    rolled = [pltpu.roll(table_ref[...], 256 - (step * 16 + 6), 1) for step in range(8)]
    for n in range(HEADS):
        at = (n % 4) * 32
        for c, (block, start) in enumerate(classes):
            parts = [spread(rolled[start - 2 * block - i + 7], n)[:, :128] for i in range(2)]
            row_a = jnp.clip(2 * block + qi - 3, 0, 9)
            row_k = start + kr
            ok = col_ok & (row_k >= row_a) & (row_k <= row_a + 6)
            bias_ref[c, n // 4, at : at + 32, :] = jnp.where(ok, jnp.concatenate(parts, axis=0), NEG)


def group_bias_call(table):
    return pl.pallas_call(
        group_bias_kernel,
        in_specs=[VM],
        out_specs=VM,
        out_shape=pltpu.HBM((5, 4, 128, 128), F32),
        compiler_params=pltpu.CompilerParams(vmem_limit_bytes=SMALL),
        cost_estimate=pl.CostEstimate(flops=4_000_000, transcendentals=0, bytes_accessed=1_300_000),
        name="group_bias",
    )(table)


def fetch_weights(layer, far, near, sems):
    copies = [pltpu.make_async_copy(a.at[layer], b, sems.at[i]) for i, (a, b) in enumerate(zip(far, near))]
    for c in copies:
        c.start()
    return copies


WEIGHT_SCRATCH = [
    pltpu.VMEM((512, 512), BF16),
    pltpu.VMEM((512, 2048), BF16),
    pltpu.VMEM((2048, 512), BF16),
    pltpu.SemaphoreType.DMA((3,)),
]


def send_rows(done, stage, pieces):
    for at, block, slot in pieces:
        for f in range(4):
            stage[pl.ds(block * 256 + slot * 4 + f, 16, stride=16), :] = done[at : at + 16, f * 128 : (f + 1) * 128]


def local_kernel(
    xpad_ref, x_ref, q_ref, gains_ref, bias, wqkv, wp_far, wu_far, wd_far, out_ref,
    k_s, v_s, a_s, stage, wp, wu, wd, sems,
):
    copies = fetch_weights(0, (wp_far, wu_far, wd_far), (wp, wu, wd), sems)
    k_s[912:928, :] = jnp.zeros((16, 512), BF16)
    v_s[...] = jnp.ones((928, 1024), BF16)
    for g in range(4):
        v_s[912:928, g * 256 : g * 256 + 128] = jnp.zeros((16, 128), BF16)
    for r in range(3):
        rows = slice(r * 304, (r + 1) * 304)
        normed = layer_norm(xpad_ref[rows, :], gains_ref[0:1, :])
        k_s[rows, :] = dot(normed, wqkv[0, :, 512:1024]).astype(BF16)
        value = dot(normed, wqkv[0, :, 1024:]).astype(BF16)
        for g in range(4):
            v_s[rows, g * 256 : g * 256 + 128] = value[:, g * 128 : (g + 1) * 128]

    def attend(b, carry):
        at_q = b * 64
        at_k = b * 96
        kind = 0 if b == 0 else 2 if b == 7 else 1
        outs = attend_units(
            [
                (
                    q_ref[pl.ds(at_q, 64), g * 128 : (g + 1) * 128],
                    k_s[pl.ds(at_k, 256), g * 128 : (g + 1) * 128],
                    v_s[pl.ds(at_k, 256), g * 256 : (g + 1) * 256],
                    bias[kind, g],
                )
                for g in range(4)
            ]
        )
        for g in range(4):
            a_s[pl.ds(at_q, 64), g * 128 : (g + 1) * 128] = outs[g]
        return carry

    for b in range(8):
        attend(b, 0)
    for c in copies:
        c.wait()
    for half in range(2):
        rows = slice(half * 256, (half + 1) * 256)
        done = finish_rows(a_s[rows, :], x_ref[rows, :], gains_ref[1:2, :], wp, wu, wd)
        send_rows(done, stage, [((2 * r + g) * 16, r, g * 2 + half) for r in range(8) for g in range(2)])
    out_ref[...] = stage[...].reshape(128, 16, 128).astype(BF16)


def local_call(xpad, x, q, gains, bias, wqkv, wp, wu, wd):
    return pl.pallas_call(
        local_kernel,
        in_specs=[VM] * 6 + [FAR] * 3,
        out_specs=VM,
        out_shape=pltpu.HBM((128, 16, 128), BF16),
        scratch_shapes=[
            pltpu.VMEM((928, 512), BF16),
            pltpu.VMEM((928, 1024), BF16),
            pltpu.VMEM((512, 512), BF16),
            pltpu.VMEM((2048, 128), F32),
        ]
        + WEIGHT_SCRATCH,
        compiler_params=pltpu.CompilerParams(vmem_limit_bytes=BIG),
        cost_estimate=pl.CostEstimate(flops=8_000_000_000, transcendentals=3_000_000, bytes_accessed=12_000_000),
        name="local_layer",
    )(xpad, x, q, gains, bias, wqkv, wp, wu, wd)


def group_kernel(
    in_ref, gains_ref, bias_far, wqkv, wp_far, wu_far, wd_far, out_ref,
    x_s, q_s, k_s, v_s, a_s, stage, wp, wu, wd, sems, bias, bias_sem,
):
    bias_copy = pltpu.make_async_copy(bias_far, bias, bias_sem)
    bias_copy.start()
    copies = fetch_weights(1, (wp_far, wu_far, wd_far), (wp, wu, wd), sems)
    stage[...] = in_ref[...].astype(F32).reshape(2048, 128)
    for g in range(2):
        for p in range(16):
            r, half = p // 2, p % 2
            at = g * 256 + p * 16
            for f in range(4):
                x_s[at : at + 16, f * 128 : (f + 1) * 128] = stage[
                    pl.ds(r * 256 + (g * 2 + half) * 4 + f, 16, stride=16), :
                ]
    v_s[...] = jnp.ones((512, 1024), BF16)
    for g in range(2):
        rows = slice(g * 256, (g + 1) * 256)
        normed = layer_norm(x_s[rows, :], gains_ref[2:3, :])
        q_s[rows, :] = (dot(normed, wqkv[1, :, :512]) * QSCALE).astype(BF16)
        k_s[rows, :] = dot(normed, wqkv[1, :, 512:1024]).astype(BF16)
        value = dot(normed, wqkv[1, :, 1024:]).astype(BF16)
        for h in range(4):
            v_s[rows, h * 256 : h * 256 + 128] = value[:, h * 128 : (h + 1) * 128]

    bias_copy.wait()

    def attend(b, carry):
        start = min(max(2 * b - 3, 0), 8)
        kind = b if b < 2 else 2 if b < 6 else b - 3
        units = []
        for g in range(2):
            at_q = g * 256 + b * 32
            at_k = g * 256 + start * 16
            for h in range(4):
                units.append(
                    (
                        q_s[pl.ds(at_q, 32), h * 128 : (h + 1) * 128],
                        k_s[pl.ds(at_k, 128), h * 128 : (h + 1) * 128],
                        v_s[pl.ds(at_k, 128), h * 256 : (h + 1) * 256],
                        bias[kind, h],
                    )
                )
        outs = attend_units(units)
        for g in range(2):
            at_q = g * 256 + b * 32
            for h in range(4):
                a_s[pl.ds(at_q, 32), h * 128 : (h + 1) * 128] = outs[g * 4 + h]
        return carry

    for b in range(8):
        attend(b, 0)
    for c in copies:
        c.wait()
    for g in range(2):
        rows = slice(g * 256, (g + 1) * 256)
        done = finish_rows(a_s[rows, :], x_s[rows, :], gains_ref[3:4, :], wp, wu, wd)
        send_rows(done, stage, [(p * 16, p // 2, g * 2 + p % 2) for p in range(16)])
    out_ref[...] = stage[...].reshape(128, 16, 128).astype(BF16)


def group_call(rows, gains, bias, wqkv, wp, wu, wd):
    return pl.pallas_call(
        group_kernel,
        in_specs=[VM, VM, FAR, VM] + [FAR] * 3,
        out_specs=VM,
        out_shape=pltpu.VMEM((128, 16, 128), BF16),
        scratch_shapes=[
            pltpu.VMEM((512, 512), F32),
            pltpu.VMEM((512, 512), BF16),
            pltpu.VMEM((512, 512), BF16),
            pltpu.VMEM((512, 1024), BF16),
            pltpu.VMEM((512, 512), BF16),
            pltpu.VMEM((2048, 128), F32),
        ]
        + WEIGHT_SCRATCH
        + [pltpu.VMEM((5, 4, 128, 128), F32), pltpu.SemaphoreType.DMA(())],
        compiler_params=pltpu.CompilerParams(vmem_limit_bytes=BIG),
        cost_estimate=pl.CostEstimate(flops=7_000_000_000, transcendentals=3_000_000, bytes_accessed=10_000_000),
        name="group_layer",
    )(rows, gains, bias, wqkv, wp, wu, wd)


def place_kernel(in_ref, out_ref, stage):
    stage[...] = in_ref[...].astype(F32).reshape(2048, 128)
    for r in range(8):
        for slot in range(4):
            parts = [stage[pl.ds(r * 256 + slot * 4 + f, 16, stride=16), :] for f in range(4)]
            out_ref[slot % 2 * 16 + 2 * r + slot // 2] = jnp.concatenate(parts, axis=1).astype(BF16)


def place_call(rows):
    return pl.pallas_call(
        place_kernel,
        in_specs=[VM],
        out_specs=VM,
        out_shape=jax.ShapeDtypeStruct((TR, TC, D), BF16),
        scratch_shapes=[pltpu.VMEM((2048, 128), F32)],
        compiler_params=pltpu.CompilerParams(vmem_limit_bytes=SMALL),
        name="place",
    )(rows)


def edges(cells, axis, dim):
    count = lax.axis_size(axis)
    ends = count - 1
    size = cells.shape[dim]
    head = lax.slice_in_dim(cells, 0, 3, axis=dim)
    tail = lax.slice_in_dim(cells, size - 3, size, axis=dim)
    before = lax.ppermute(tail, axis, [(i, i + 1) for i in range(ends)])
    after = lax.ppermute(head, axis, [(i + 1, i) for i in range(ends)])
    return before, after


def exchange(rows):
    return lax.all_to_all(rows, ("row", "col"), 0, 0, tiled=True)


def body(tokens, norm_gains, qkv_weight, rel_bias, proj_weight, up_weight, down_weight):
    x = tokens.reshape(TR * TC, D)
    top, bottom = edges(tokens, "row", 0)
    tall = jnp.concatenate([top, tokens, bottom], axis=0)
    left, right = edges(tall, "col", 1)
    xpad = jnp.concatenate([left, tall, right, jnp.zeros((TR + 6, 2, D), BF16)], axis=1)
    xpad = xpad.reshape((TR + 6) * 24, D)

    table = rel_bias * LOG2E
    local_table = jnp.pad(table[0], ((0, 0), (0, 0), (0, 11))).reshape(HEADS, 312)
    local_table = jnp.pad(local_table, ((0, 0), (0, 200)))
    group_table = jnp.pad(table[1], ((0, 0), (1, 2), (0, 3))).reshape(HEADS, 256)
    place = jnp.stack([lax.axis_index("row") * TR, lax.axis_index("col") * TC]).astype(jnp.int32)

    near = lambda a: pltpu.with_memory_space_constraint(a, pltpu.VMEM)
    far = lambda a: pltpu.with_memory_space_constraint(a, pltpu.HBM)
    wqkv, wp, wu, wd = near(qkv_weight), far(proj_weight), far(up_weight), far(down_weight)
    x = near(x)
    q = query_call(x, norm_gains, wqkv)
    local_bias = local_bias_call(place, local_table)
    group_bias = group_bias_call(group_table)
    sent = local_call(near(xpad), x, q, norm_gains, local_bias, wqkv, wp, wu, wd)
    got = exchange(sent)
    back = group_call(near(got), norm_gains, group_bias, wqkv, wp, wu, wd)
    return place_call(near(exchange(back)))


def solution(mesh):
    placed = (P("row", "col", None), P(), P(), P(), P(), P(), P())
    return jax.shard_map(
        body, mesh=mesh, in_specs=placed, out_specs=P("row", "col", None), check_vma=False
    )
```

```python
import jax
import jax.numpy as jnp
from jax import lax
from jax.experimental import pallas as pl
from jax.experimental.pallas import tpu as pltpu
from jax.sharding import PartitionSpec as P

D = 512
HEADS = 16
FF = 2048
TR = 32
TC = 16
MAP = 256
LOG2E = 1.4426950408889634
QSCALE = LOG2E * 32.0 ** -0.5
NEG = -1e30
F32 = jnp.float32
BF16 = jnp.bfloat16
BIG = 24 * 1024 * 1024
SMALL = 12 * 1024 * 1024
VM = pl.BlockSpec(memory_space=pltpu.VMEM)
FAR = pl.BlockSpec(memory_space=pltpu.HBM)


def iota(shape, dim):
    return lax.broadcasted_iota(jnp.int32, shape, dim)


def layer_norm(rows, gain):
    x = rows.astype(F32)
    centred = x - jnp.mean(x, axis=-1, keepdims=True)
    variance = jnp.mean(centred * centred, axis=-1, keepdims=True)
    return (centred * lax.rsqrt(variance + 1e-5) * gain).astype(BF16)


def dot(a, b):
    return jnp.dot(a, b, preferred_element_type=F32)


def dot_t(a, b):
    return lax.dot_general(a, b, (((1,), (1,)), ((), ())), preferred_element_type=F32)


def gelu(z):
    inner = 0.7978845608028654 * (z + 0.044715 * (z * z * z))
    return 0.5 * z * (1.0 + jnp.tanh(inner))


def head_masks(count):
    lane = iota((count, 128), 1) // 32
    return [lane == h for h in range(4)]


def attend_units(units):
    n = units[0][0].shape[0]
    masks = head_masks(n)
    zero = jnp.zeros((n, 128), BF16)
    scores = []
    for q, k, _, bias in units:
        stacked = jnp.concatenate([jnp.where(m, q, zero) for m in masks], axis=0)
        scores.append(dot_t(stacked, k) + bias)
    tops = [jnp.max(s, axis=-1, keepdims=True) for s in scores]
    probs = [jnp.exp2(s - t).astype(BF16) for s, t in zip(scores, tops)]
    outs = []
    for unit, p in zip(units, probs):
        both = dot(p, unit[2])
        top, low = both[:n, :128], both[:n, 128:]
        for h in range(1, 4):
            part = both[h * n : (h + 1) * n]
            top = jnp.where(masks[h], part[:, :128], top)
            low = jnp.where(masks[h], part[:, 128:], low)
        outs.append((top / low).astype(BF16))
    return outs


def finish_rows(attended, stream, gain, wp, wu, wd):
    mixed = (dot(attended, wp[...]) + stream.astype(F32)).astype(BF16)
    normed = layer_norm(mixed, gain)
    acc = mixed.astype(F32)
    for c in range(2):
        hidden = gelu(dot(normed, wu[:, c * 1024 : (c + 1) * 1024])).astype(BF16)
        acc = acc + dot(hidden, wd[c * 1024 : (c + 1) * 1024, :])
    return acc


def query_kernel(x_ref, gains_ref, w_ref, q_ref):
    for half in range(2):
        rows = slice(half * 256, (half + 1) * 256)
        normed = layer_norm(x_ref[rows, :], gains_ref[0:1, :])
        q_ref[rows, :] = (dot(normed, w_ref[0, :, :512]) * QSCALE).astype(BF16)


def query_call(x, gains, wqkv):
    return pl.pallas_call(
        query_kernel,
        in_specs=[VM] * 3,
        out_specs=VM,
        out_shape=pltpu.VMEM((512, 512), BF16),
        compiler_params=pltpu.CompilerParams(vmem_limit_bytes=SMALL),
        cost_estimate=pl.CostEstimate(flops=2 * 512 ** 3, transcendentals=0, bytes_accessed=3 * 512 * 1024),
        name="query",
    )(x, gains, wqkv)


def spread(table, n):
    base = jnp.broadcast_to(table[n : n + 1, :], (16, table.shape[1]))
    return pltpu.roll(base, 0, 1, stride=1, stride_axis=0)


def local_bias_kernel(place_ref, table_ref, bias_ref):
    first_row = place_ref[0]
    first_col = place_ref[1]
    row = iota((64, 256), 0)
    lane = iota((64, 256), 1)
    qi = row // 16
    qj = row % 16
    kr = lane // 24
    kc = lane - kr * 24
    col_q = first_col + qj
    col_a = jnp.clip(col_q - 3, 0, MAP - 7)
    col_k = first_col + kc - 3
    col_ok = (col_k >= col_a) & (col_k <= col_a + 6)
    oks = []
    for block in (0, 1, 7):
        row_q = first_row + 4 * block + qi
        row_a = jnp.clip(row_q - 3, 0, MAP - 7)
        row_k = first_row + 4 * block - 3 + kr
        oks.append(col_ok & (row_k >= row_a) & (row_k <= row_a + 6))
    rolled = [pltpu.roll(table_ref[...], 512 - (24 * (3 - i) + 3), 1) for i in range(4)]
    for n in range(HEADS):
        parts = [spread(rolled[i], n)[:, :256] for i in range(4)]
        full = jnp.concatenate(parts, axis=0)
        at = (n % 4) * 64
        for c in range(3):
            bias_ref[c, n // 4, at : at + 64, :] = jnp.where(oks[c], full, NEG)


def local_bias_call(place, table):
    return pl.pallas_call(
        local_bias_kernel,
        in_specs=[pl.BlockSpec(memory_space=pltpu.SMEM), VM],
        out_specs=VM,
        out_shape=pltpu.VMEM((3, 4, 256, 256), F32),
        compiler_params=pltpu.CompilerParams(vmem_limit_bytes=SMALL),
        cost_estimate=pl.CostEstimate(flops=4_000_000, transcendentals=0, bytes_accessed=3 * 1024 * 1024),
        name="local_bias",
    )(place, table)


def group_bias_kernel(table_ref, bias_ref):
    row = iota((32, 128), 0)
    lane = iota((32, 128), 1)
    qi = row // 16
    qj = row % 16
    kr = lane // 16
    kc = lane % 16
    col_a = jnp.clip(qj - 3, 0, 9)
    col_ok = (kc >= col_a) & (kc <= col_a + 6)
    classes = ((0, 0), (1, 0), (2, 1), (6, 8), (7, 8))
    rolled = [pltpu.roll(table_ref[...], 256 - (step * 16 + 6), 1) for step in range(8)]
    for n in range(HEADS):
        at = (n % 4) * 32
        for c, (block, start) in enumerate(classes):
            parts = [spread(rolled[start - 2 * block - i + 7], n)[:, :128] for i in range(2)]
            row_a = jnp.clip(2 * block + qi - 3, 0, 9)
            row_k = start + kr
            ok = col_ok & (row_k >= row_a) & (row_k <= row_a + 6)
            bias_ref[c, n // 4, at : at + 32, :] = jnp.where(ok, jnp.concatenate(parts, axis=0), NEG)


def group_bias_call(table):
    return pl.pallas_call(
        group_bias_kernel,
        in_specs=[VM],
        out_specs=VM,
        out_shape=pltpu.VMEM((5, 4, 128, 128), F32),
        compiler_params=pltpu.CompilerParams(vmem_limit_bytes=SMALL),
        cost_estimate=pl.CostEstimate(flops=4_000_000, transcendentals=0, bytes_accessed=1_300_000),
        name="group_bias",
    )(table)


def fetch_weights(layer, far, near, sems):
    copies = [pltpu.make_async_copy(a.at[layer], b, sems.at[i]) for i, (a, b) in enumerate(zip(far, near))]
    for c in copies:
        c.start()
    return copies


WEIGHT_SCRATCH = [
    pltpu.VMEM((512, 512), BF16),
    pltpu.VMEM((512, 2048), BF16),
    pltpu.VMEM((2048, 512), BF16),
    pltpu.SemaphoreType.DMA((3,)),
]


def send_rows(done, stage, pieces):
    for at, block, slot in pieces:
        for f in range(4):
            stage[pl.ds(block * 256 + slot * 4 + f, 16, stride=16), :] = done[at : at + 16, f * 128 : (f + 1) * 128]


def local_kernel(
    xpad_ref, x_ref, q_ref, gains_ref, bias, wqkv, wp_far, wu_far, wd_far, out_ref,
    k_s, v_s, a_s, stage, wp, wu, wd, sems,
):
    copies = fetch_weights(0, (wp_far, wu_far, wd_far), (wp, wu, wd), sems)
    k_s[912:928, :] = jnp.zeros((16, 512), BF16)
    v_s[...] = jnp.ones((928, 1024), BF16)
    for g in range(4):
        v_s[912:928, g * 256 : g * 256 + 128] = jnp.zeros((16, 128), BF16)
    for r in range(3):
        rows = slice(r * 304, (r + 1) * 304)
        normed = layer_norm(xpad_ref[rows, :], gains_ref[0:1, :])
        k_s[rows, :] = dot(normed, wqkv[0, :, 512:1024]).astype(BF16)
        value = dot(normed, wqkv[0, :, 1024:]).astype(BF16)
        for g in range(4):
            v_s[rows, g * 256 : g * 256 + 128] = value[:, g * 128 : (g + 1) * 128]

    def attend(b, carry):
        at_q = b * 64
        at_k = b * 96
        kind = 0 if b == 0 else 2 if b == 7 else 1
        outs = attend_units(
            [
                (
                    q_ref[pl.ds(at_q, 64), g * 128 : (g + 1) * 128],
                    k_s[pl.ds(at_k, 256), g * 128 : (g + 1) * 128],
                    v_s[pl.ds(at_k, 256), g * 256 : (g + 1) * 256],
                    bias[kind, g],
                )
                for g in range(4)
            ]
        )
        for g in range(4):
            a_s[pl.ds(at_q, 64), g * 128 : (g + 1) * 128] = outs[g]
        return carry

    for b in range(8):
        attend(b, 0)
    for c in copies:
        c.wait()
    done = finish_rows(a_s[...], x_ref[...], gains_ref[1:2, :], wp, wu, wd)
    send_rows(done, stage, [(i * 16, i % 16 // 2, i % 2 * 2 + i // 16) for i in range(32)])
    out_ref[...] = stage[...].reshape(128, 16, 128).astype(BF16)


def local_call(xpad, x, q, gains, bias, wqkv, wp, wu, wd):
    return pl.pallas_call(
        local_kernel,
        in_specs=[VM] * 6 + [FAR] * 3,
        out_specs=VM,
        out_shape=pltpu.VMEM((128, 16, 128), BF16),
        scratch_shapes=[
            pltpu.VMEM((928, 512), BF16),
            pltpu.VMEM((928, 1024), BF16),
            pltpu.VMEM((512, 512), BF16),
            pltpu.VMEM((2048, 128), F32),
        ]
        + WEIGHT_SCRATCH,
        compiler_params=pltpu.CompilerParams(vmem_limit_bytes=BIG),
        cost_estimate=pl.CostEstimate(flops=8_000_000_000, transcendentals=3_000_000, bytes_accessed=12_000_000),
        name="local_layer",
    )(xpad, x, q, gains, bias, wqkv, wp, wu, wd)


def group_kernel(
    in_ref, gains_ref, bias, wqkv, wp_far, wu_far, wd_far, out_ref,
    x_s, q_s, k_s, v_s, a_s, stage, wp, wu, wd, sems,
):
    copies = fetch_weights(1, (wp_far, wu_far, wd_far), (wp, wu, wd), sems)
    stage[...] = in_ref[...].astype(F32).reshape(2048, 128)
    for g in range(2):
        for p in range(16):
            r, half = p // 2, p % 2
            at = g * 256 + p * 16
            for f in range(4):
                x_s[at : at + 16, f * 128 : (f + 1) * 128] = stage[
                    pl.ds(r * 256 + (g * 2 + half) * 4 + f, 16, stride=16), :
                ]
    v_s[...] = jnp.ones((512, 1024), BF16)
    for g in range(2):
        rows = slice(g * 256, (g + 1) * 256)
        normed = layer_norm(x_s[rows, :], gains_ref[2:3, :])
        q_s[rows, :] = (dot(normed, wqkv[1, :, :512]) * QSCALE).astype(BF16)
        k_s[rows, :] = dot(normed, wqkv[1, :, 512:1024]).astype(BF16)
        value = dot(normed, wqkv[1, :, 1024:]).astype(BF16)
        for h in range(4):
            v_s[rows, h * 256 : h * 256 + 128] = value[:, h * 128 : (h + 1) * 128]

    def attend(b, carry):
        start = min(max(2 * b - 3, 0), 8)
        kind = b if b < 2 else 2 if b < 6 else b - 3
        units = []
        for g in range(2):
            at_q = g * 256 + b * 32
            at_k = g * 256 + start * 16
            for h in range(4):
                units.append(
                    (
                        q_s[pl.ds(at_q, 32), h * 128 : (h + 1) * 128],
                        k_s[pl.ds(at_k, 128), h * 128 : (h + 1) * 128],
                        v_s[pl.ds(at_k, 128), h * 256 : (h + 1) * 256],
                        bias[kind, h],
                    )
                )
        outs = attend_units(units)
        for g in range(2):
            at_q = g * 256 + b * 32
            for h in range(4):
                a_s[pl.ds(at_q, 32), h * 128 : (h + 1) * 128] = outs[g * 4 + h]
        return carry

    for b in range(8):
        attend(b, 0)
    for c in copies:
        c.wait()
    done = finish_rows(a_s[...], x_s[...], gains_ref[3:4, :], wp, wu, wd)
    send_rows(done, stage, [(i * 16, i % 16 // 2, i // 16 * 2 + i % 2) for i in range(32)])
    out_ref[...] = stage[...].reshape(128, 16, 128).astype(BF16)


def group_call(rows, gains, bias, wqkv, wp, wu, wd):
    return pl.pallas_call(
        group_kernel,
        in_specs=[VM] * 4 + [FAR] * 3,
        out_specs=VM,
        out_shape=pltpu.VMEM((128, 16, 128), BF16),
        scratch_shapes=[
            pltpu.VMEM((512, 512), F32),
            pltpu.VMEM((512, 512), BF16),
            pltpu.VMEM((512, 512), BF16),
            pltpu.VMEM((512, 1024), BF16),
            pltpu.VMEM((512, 512), BF16),
            pltpu.VMEM((2048, 128), F32),
        ]
        + WEIGHT_SCRATCH,
        compiler_params=pltpu.CompilerParams(vmem_limit_bytes=BIG),
        cost_estimate=pl.CostEstimate(flops=7_000_000_000, transcendentals=3_000_000, bytes_accessed=10_000_000),
        name="group_layer",
    )(rows, gains, bias, wqkv, wp, wu, wd)


def place_kernel(in_ref, out_ref, stage):
    stage[...] = in_ref[...].astype(F32).reshape(2048, 128)
    for r in range(8):
        for slot in range(4):
            parts = [stage[pl.ds(r * 256 + slot * 4 + f, 16, stride=16), :] for f in range(4)]
            out_ref[slot % 2 * 16 + 2 * r + slot // 2] = jnp.concatenate(parts, axis=1).astype(BF16)


def place_call(rows):
    return pl.pallas_call(
        place_kernel,
        in_specs=[VM],
        out_specs=VM,
        out_shape=jax.ShapeDtypeStruct((TR, TC, D), BF16),
        scratch_shapes=[pltpu.VMEM((2048, 128), F32)],
        compiler_params=pltpu.CompilerParams(vmem_limit_bytes=SMALL),
        name="place",
    )(rows)


def edges(cells, axis, dim):
    count = lax.axis_size(axis)
    ends = count - 1
    size = cells.shape[dim]
    head = lax.slice_in_dim(cells, 0, 3, axis=dim)
    tail = lax.slice_in_dim(cells, size - 3, size, axis=dim)
    before = lax.ppermute(tail, axis, [(i, i + 1) for i in range(ends)])
    after = lax.ppermute(head, axis, [(i + 1, i) for i in range(ends)])
    return before, after


def exchange(rows):
    return lax.all_to_all(rows, ("row", "col"), 0, 0, tiled=True)


def body(tokens, norm_gains, qkv_weight, rel_bias, proj_weight, up_weight, down_weight):
    x = tokens.reshape(TR * TC, D)
    top, bottom = edges(tokens, "row", 0)
    tall = jnp.concatenate([top, tokens, bottom], axis=0)
    left, right = edges(tall, "col", 1)
    xpad = jnp.concatenate([left, tall, right, jnp.zeros((TR + 6, 2, D), BF16)], axis=1)
    xpad = xpad.reshape((TR + 6) * 24, D)

    table = rel_bias * LOG2E
    local_table = jnp.pad(table[0], ((0, 0), (0, 0), (0, 11))).reshape(HEADS, 312)
    local_table = jnp.pad(local_table, ((0, 0), (0, 200)))
    group_table = jnp.pad(table[1], ((0, 0), (1, 2), (0, 3))).reshape(HEADS, 256)
    place = jnp.stack([lax.axis_index("row") * TR, lax.axis_index("col") * TC]).astype(jnp.int32)

    near = lambda a: pltpu.with_memory_space_constraint(a, pltpu.VMEM)
    far = lambda a: pltpu.with_memory_space_constraint(a, pltpu.HBM)
    wqkv, wp, wu, wd = near(qkv_weight), far(proj_weight), far(up_weight), far(down_weight)
    x = near(x)
    q = query_call(x, norm_gains, wqkv)
    local_bias = local_bias_call(place, local_table)
    group_bias = group_bias_call(group_table)
    xpad, group_bias = lax.optimization_barrier((xpad, group_bias))
    sent = local_call(near(xpad), x, q, norm_gains, local_bias, wqkv, wp, wu, wd)
    got = exchange(sent)
    back = group_call(near(got), norm_gains, near(group_bias), wqkv, wp, wu, wd)
    return place_call(near(exchange(back)))


def solution(mesh):
    placed = (P("row", "col", None), P(), P(), P(), P(), P(), P())
    return jax.shard_map(
        body, mesh=mesh, in_specs=placed, out_specs=P("row", "col", None), check_vma=False
    )
```

```python
import jax
import jax.numpy as jnp
from jax import lax
from jax.experimental import pallas as pl
from jax.experimental.pallas import tpu as pltpu
from jax.sharding import PartitionSpec as P

D = 512
HEADS = 16
FF = 2048
TR = 32
TC = 16
MAP = 256
LOG2E = 1.4426950408889634
QSCALE = LOG2E * 32.0 ** -0.5
NEG = -1e30
F32 = jnp.float32
BF16 = jnp.bfloat16
BIG = 24 * 1024 * 1024
SMALL = 12 * 1024 * 1024
VM = pl.BlockSpec(memory_space=pltpu.VMEM)
FAR = pl.BlockSpec(memory_space=pltpu.HBM)


def iota(shape, dim):
    return lax.broadcasted_iota(jnp.int32, shape, dim)


def layer_norm(rows, gain):
    x = rows.astype(F32)
    centred = x - jnp.mean(x, axis=-1, keepdims=True)
    variance = jnp.mean(centred * centred, axis=-1, keepdims=True)
    return (centred * lax.rsqrt(variance + 1e-5) * gain).astype(BF16)


def dot(a, b):
    return jnp.dot(a, b, preferred_element_type=F32)


def dot_t(a, b):
    return lax.dot_general(a, b, (((1,), (1,)), ((), ())), preferred_element_type=F32)


def gelu(z):
    inner = 0.7978845608028654 * (z + 0.044715 * (z * z * z))
    return 0.5 * z * (1.0 + jnp.tanh(inner))


def head_masks(count):
    lane = iota((count, 128), 1) // 32
    return [lane == h for h in range(4)]


def attend_units(units):
    n = units[0][0].shape[0]
    masks = head_masks(n)
    zero = jnp.zeros((n, 128), BF16)
    scores = []
    for q, k, _, bias in units:
        stacked = jnp.concatenate([jnp.where(m, q, zero) for m in masks], axis=0)
        scores.append(dot_t(stacked, k) + bias)
    tops = [jnp.max(s, axis=-1, keepdims=True) for s in scores]
    probs = [jnp.exp2(s - t).astype(BF16) for s, t in zip(scores, tops)]
    outs = []
    for unit, p in zip(units, probs):
        both = dot(p, unit[2])
        top, low = both[:n, :128], both[:n, 128:]
        for h in range(1, 4):
            part = both[h * n : (h + 1) * n]
            top = jnp.where(masks[h], part[:, :128], top)
            low = jnp.where(masks[h], part[:, 128:], low)
        outs.append((top / low).astype(BF16))
    return outs


def finish_rows(attended, stream, gain, wp, wu, wd):
    mixed = (dot(attended, wp[...]) + stream.astype(F32)).astype(BF16)
    normed = layer_norm(mixed, gain)
    acc = mixed.astype(F32)
    for c in range(2):
        hidden = gelu(dot(normed, wu[:, c * 1024 : (c + 1) * 1024])).astype(BF16)
        acc = acc + dot(hidden, wd[c * 1024 : (c + 1) * 1024, :])
    return acc


def query_kernel(x_ref, gains_ref, w_ref, q_ref):
    for half in range(2):
        rows = slice(half * 256, (half + 1) * 256)
        normed = layer_norm(x_ref[rows, :], gains_ref[0:1, :])
        q_ref[rows, :] = (dot(normed, w_ref[0, :, :512]) * QSCALE).astype(BF16)


def query_call(x, gains, wqkv):
    return pl.pallas_call(
        query_kernel,
        in_specs=[VM] * 3,
        out_specs=VM,
        out_shape=pltpu.VMEM((512, 512), BF16),
        compiler_params=pltpu.CompilerParams(vmem_limit_bytes=SMALL),
        cost_estimate=pl.CostEstimate(flops=2 * 512 ** 3, transcendentals=0, bytes_accessed=3 * 512 * 1024),
        name="query",
    )(x, gains, wqkv)


def spread(table, n):
    base = jnp.broadcast_to(table[n : n + 1, :], (16, table.shape[1]))
    return pltpu.roll(base, 0, 1, stride=1, stride_axis=0)


def local_bias_kernel(place_ref, table_ref, bias_ref):
    first_row = place_ref[0]
    first_col = place_ref[1]
    row = iota((64, 256), 0)
    lane = iota((64, 256), 1)
    qi = row // 16
    qj = row % 16
    kr = lane // 24
    kc = lane - kr * 24
    col_q = first_col + qj
    col_a = jnp.clip(col_q - 3, 0, MAP - 7)
    col_k = first_col + kc - 3
    col_ok = (col_k >= col_a) & (col_k <= col_a + 6)
    oks = []
    for block in (0, 1, 7):
        row_q = first_row + 4 * block + qi
        row_a = jnp.clip(row_q - 3, 0, MAP - 7)
        row_k = first_row + 4 * block - 3 + kr
        oks.append(col_ok & (row_k >= row_a) & (row_k <= row_a + 6))
    rolled = [pltpu.roll(table_ref[...], 512 - (24 * (3 - i) + 3), 1) for i in range(4)]
    for n in range(HEADS):
        parts = [spread(rolled[i], n)[:, :256] for i in range(4)]
        full = jnp.concatenate(parts, axis=0)
        at = (n % 4) * 64
        for c in range(3):
            bias_ref[c, n // 4, at : at + 64, :] = jnp.where(oks[c], full, NEG)


def local_bias_call(place, table):
    return pl.pallas_call(
        local_bias_kernel,
        in_specs=[pl.BlockSpec(memory_space=pltpu.SMEM), VM],
        out_specs=VM,
        out_shape=pltpu.VMEM((3, 4, 256, 256), F32),
        compiler_params=pltpu.CompilerParams(vmem_limit_bytes=SMALL),
        cost_estimate=pl.CostEstimate(flops=4_000_000, transcendentals=0, bytes_accessed=3 * 1024 * 1024),
        name="local_bias",
    )(place, table)


def group_bias_kernel(table_ref, bias_ref):
    row = iota((32, 128), 0)
    lane = iota((32, 128), 1)
    qi = row // 16
    qj = row % 16
    kr = lane // 16
    kc = lane % 16
    col_a = jnp.clip(qj - 3, 0, 9)
    col_ok = (kc >= col_a) & (kc <= col_a + 6)
    classes = ((0, 0), (1, 0), (2, 1), (6, 8), (7, 8))
    rolled = [pltpu.roll(table_ref[...], 256 - (step * 16 + 6), 1) for step in range(8)]
    for n in range(HEADS):
        at = (n % 4) * 32
        for c, (block, start) in enumerate(classes):
            parts = [spread(rolled[start - 2 * block - i + 7], n)[:, :128] for i in range(2)]
            row_a = jnp.clip(2 * block + qi - 3, 0, 9)
            row_k = start + kr
            ok = col_ok & (row_k >= row_a) & (row_k <= row_a + 6)
            bias_ref[c, n // 4, at : at + 32, :] = jnp.where(ok, jnp.concatenate(parts, axis=0), NEG)


def group_bias_call(table):
    return pl.pallas_call(
        group_bias_kernel,
        in_specs=[VM],
        out_specs=VM,
        out_shape=pltpu.VMEM((5, 4, 128, 128), F32),
        compiler_params=pltpu.CompilerParams(vmem_limit_bytes=SMALL),
        cost_estimate=pl.CostEstimate(flops=4_000_000, transcendentals=0, bytes_accessed=1_300_000),
        name="group_bias",
    )(table)


def fetch_weights(layer, far, near, sems):
    copies = [pltpu.make_async_copy(a.at[layer], b, sems.at[i]) for i, (a, b) in enumerate(zip(far, near))]
    for c in copies:
        c.start()
    return copies


WEIGHT_SCRATCH = [
    pltpu.VMEM((512, 512), BF16),
    pltpu.VMEM((512, 2048), BF16),
    pltpu.VMEM((2048, 512), BF16),
    pltpu.SemaphoreType.DMA((3,)),
]


def send_rows(done, stage, pieces):
    for at, block, slot in pieces:
        for f in range(4):
            stage[pl.ds(block * 256 + slot * 4 + f, 16, stride=16), :] = done[at : at + 16, f * 128 : (f + 1) * 128]


def local_kernel(
    xpad_ref, x_ref, q_ref, gains_ref, bias, wqkv, wp_far, wu_far, wd_far, out_ref,
    k_s, v_s, a_s, stage, wp, wu, wd, sems,
):
    copies = fetch_weights(0, (wp_far, wu_far, wd_far), (wp, wu, wd), sems)
    k_s[912:928, :] = jnp.zeros((16, 512), BF16)
    v_s[...] = jnp.ones((928, 1024), BF16)
    for g in range(4):
        v_s[912:928, g * 256 : g * 256 + 128] = jnp.zeros((16, 128), BF16)
    for r in range(3):
        rows = slice(r * 304, (r + 1) * 304)
        normed = layer_norm(xpad_ref[rows, :], gains_ref[0:1, :])
        k_s[rows, :] = dot(normed, wqkv[0, :, 512:1024]).astype(BF16)
        value = dot(normed, wqkv[0, :, 1024:]).astype(BF16)
        for g in range(4):
            v_s[rows, g * 256 : g * 256 + 128] = value[:, g * 128 : (g + 1) * 128]

    def attend(b, carry):
        at_q = b * 64
        at_k = b * 96
        kind = 0 if b == 0 else 2 if b == 7 else 1
        outs = attend_units(
            [
                (
                    q_ref[pl.ds(at_q, 64), g * 128 : (g + 1) * 128],
                    k_s[pl.ds(at_k, 256), g * 128 : (g + 1) * 128],
                    v_s[pl.ds(at_k, 256), g * 256 : (g + 1) * 256],
                    bias[kind, g],
                )
                for g in range(4)
            ]
        )
        for g in range(4):
            a_s[pl.ds(at_q, 64), g * 128 : (g + 1) * 128] = outs[g]
        return carry

    for b in range(8):
        attend(b, 0)
    for c in copies:
        c.wait()
    done = finish_rows(a_s[...], x_ref[...], gains_ref[1:2, :], wp, wu, wd)
    send_rows(done, stage, [(i * 16, i % 16 // 2, i % 2 * 2 + i // 16) for i in range(32)])
    out_ref[...] = stage[...].reshape(128, 16, 128).astype(BF16)


def local_call(xpad, x, q, gains, bias, wqkv, wp, wu, wd):
    return pl.pallas_call(
        local_kernel,
        in_specs=[VM] * 6 + [FAR] * 3,
        out_specs=VM,
        out_shape=pltpu.VMEM((128, 16, 128), BF16),
        scratch_shapes=[
            pltpu.VMEM((928, 512), BF16),
            pltpu.VMEM((928, 1024), BF16),
            pltpu.VMEM((512, 512), BF16),
            pltpu.VMEM((2048, 128), F32),
        ]
        + WEIGHT_SCRATCH,
        compiler_params=pltpu.CompilerParams(vmem_limit_bytes=BIG),
        cost_estimate=pl.CostEstimate(flops=8_000_000_000, transcendentals=3_000_000, bytes_accessed=12_000_000),
        name="local_layer",
    )(xpad, x, q, gains, bias, wqkv, wp, wu, wd)


def group_kernel(
    in_ref, gains_ref, bias, wqkv, wp_far, wu_far, wd_far, out_ref,
    x_s, q_s, k_s, v_s, a_s, stage, wp, wu, wd, sems,
):
    copies = fetch_weights(1, (wp_far, wu_far, wd_far), (wp, wu, wd), sems)
    stage[...] = in_ref[...].astype(F32).reshape(2048, 128)
    for g in range(2):
        for p in range(16):
            r, half = p // 2, p % 2
            at = g * 256 + p * 16
            for f in range(4):
                x_s[at : at + 16, f * 128 : (f + 1) * 128] = stage[
                    pl.ds(r * 256 + (g * 2 + half) * 4 + f, 16, stride=16), :
                ]
    v_s[...] = jnp.ones((512, 1024), BF16)
    for g in range(2):
        rows = slice(g * 256, (g + 1) * 256)
        normed = layer_norm(x_s[rows, :], gains_ref[2:3, :])
        q_s[rows, :] = (dot(normed, wqkv[1, :, :512]) * QSCALE).astype(BF16)
        k_s[rows, :] = dot(normed, wqkv[1, :, 512:1024]).astype(BF16)
        value = dot(normed, wqkv[1, :, 1024:]).astype(BF16)
        for h in range(4):
            v_s[rows, h * 256 : h * 256 + 128] = value[:, h * 128 : (h + 1) * 128]

    def attend(b, carry):
        start = min(max(2 * b - 3, 0), 8)
        kind = b if b < 2 else 2 if b < 6 else b - 3
        units = []
        for g in range(2):
            at_q = g * 256 + b * 32
            at_k = g * 256 + start * 16
            for h in range(4):
                units.append(
                    (
                        q_s[pl.ds(at_q, 32), h * 128 : (h + 1) * 128],
                        k_s[pl.ds(at_k, 128), h * 128 : (h + 1) * 128],
                        v_s[pl.ds(at_k, 128), h * 256 : (h + 1) * 256],
                        bias[kind, h],
                    )
                )
        outs = attend_units(units)
        for g in range(2):
            at_q = g * 256 + b * 32
            for h in range(4):
                a_s[pl.ds(at_q, 32), h * 128 : (h + 1) * 128] = outs[g * 4 + h]
        return carry

    for b in range(8):
        attend(b, 0)
    for c in copies:
        c.wait()
    done = finish_rows(a_s[...], x_s[...], gains_ref[3:4, :], wp, wu, wd)
    send_rows(done, stage, [(i * 16, i % 16 // 2, i // 16 * 2 + i % 2) for i in range(32)])
    out_ref[...] = stage[...].reshape(128, 16, 128).astype(BF16)


def group_call(rows, gains, bias, wqkv, wp, wu, wd):
    return pl.pallas_call(
        group_kernel,
        in_specs=[VM] * 4 + [FAR] * 3,
        out_specs=VM,
        out_shape=pltpu.VMEM((128, 16, 128), BF16),
        scratch_shapes=[
            pltpu.VMEM((512, 512), F32),
            pltpu.VMEM((512, 512), BF16),
            pltpu.VMEM((512, 512), BF16),
            pltpu.VMEM((512, 1024), BF16),
            pltpu.VMEM((512, 512), BF16),
            pltpu.VMEM((2048, 128), F32),
        ]
        + WEIGHT_SCRATCH,
        compiler_params=pltpu.CompilerParams(vmem_limit_bytes=BIG),
        cost_estimate=pl.CostEstimate(flops=7_000_000_000, transcendentals=3_000_000, bytes_accessed=10_000_000),
        name="group_layer",
    )(rows, gains, bias, wqkv, wp, wu, wd)


def place_kernel(in_ref, out_ref, stage):
    stage[...] = in_ref[...].astype(F32).reshape(2048, 128)
    for r in range(8):
        for slot in range(4):
            parts = [stage[pl.ds(r * 256 + slot * 4 + f, 16, stride=16), :] for f in range(4)]
            out_ref[slot % 2 * 16 + 2 * r + slot // 2] = jnp.concatenate(parts, axis=1).astype(BF16)


def place_call(rows):
    return pl.pallas_call(
        place_kernel,
        in_specs=[VM],
        out_specs=VM,
        out_shape=jax.ShapeDtypeStruct((TR, TC, D), BF16),
        scratch_shapes=[pltpu.VMEM((2048, 128), F32)],
        compiler_params=pltpu.CompilerParams(vmem_limit_bytes=SMALL),
        name="place",
    )(rows)


def edges(cells, axis, dim):
    count = lax.axis_size(axis)
    size = cells.shape[dim]
    head = lax.slice_in_dim(cells, 0, 3, axis=dim)
    tail = lax.slice_in_dim(cells, size - 3, size, axis=dim)
    before = lax.ppermute(tail, axis, [(i, (i + 1) % count) for i in range(count)])
    after = lax.ppermute(head, axis, [((i + 1) % count, i) for i in range(count)])
    return before, after


def exchange(rows):
    return lax.all_to_all(rows, ("row", "col"), 0, 0, tiled=True)


def body(tokens, norm_gains, qkv_weight, rel_bias, proj_weight, up_weight, down_weight):
    x = tokens.reshape(TR * TC, D)
    left, right = edges(tokens, "col", 1)
    wide = jnp.concatenate([left, tokens, right, jnp.zeros((TR, 2, D), BF16)], axis=1)
    top, bottom = edges(wide, "row", 0)
    xpad = jnp.concatenate([top, wide, bottom], axis=0)
    xpad = xpad.reshape((TR + 6) * 24, D)

    table = rel_bias * LOG2E
    local_table = jnp.pad(table[0], ((0, 0), (0, 0), (0, 11))).reshape(HEADS, 312)
    local_table = jnp.pad(local_table, ((0, 0), (0, 200)))
    group_table = jnp.pad(table[1], ((0, 0), (1, 2), (0, 3))).reshape(HEADS, 256)
    place = jnp.stack([lax.axis_index("row") * TR, lax.axis_index("col") * TC]).astype(jnp.int32)

    near = lambda a: pltpu.with_memory_space_constraint(a, pltpu.VMEM)
    far = lambda a: pltpu.with_memory_space_constraint(a, pltpu.HBM)
    wqkv, wp, wu, wd = near(qkv_weight), far(proj_weight), far(up_weight), far(down_weight)
    x = near(x)
    q = query_call(x, norm_gains, wqkv)
    local_bias = local_bias_call(place, local_table)
    group_bias = group_bias_call(group_table)
    xpad, group_bias = lax.optimization_barrier((xpad, group_bias))
    sent = local_call(near(xpad), x, q, norm_gains, local_bias, wqkv, wp, wu, wd)
    got = exchange(sent)
    back = group_call(near(got), norm_gains, near(group_bias), wqkv, wp, wu, wd)
    return place_call(near(exchange(back)))


def solution(mesh):
    placed = (P("row", "col", None), P(), P(), P(), P(), P(), P())
    return jax.shard_map(
        body, mesh=mesh, in_specs=placed, out_specs=P("row", "col", None), check_vma=False
    )
```

```python
import jax
import jax.numpy as jnp
from jax import lax
from jax.experimental import pallas as pl
from jax.experimental.pallas import tpu as pltpu
from jax.sharding import PartitionSpec as P

D = 512
HEADS = 16
FF = 2048
TR = 32
TC = 16
MAP = 256
LOG2E = 1.4426950408889634
QSCALE = LOG2E * 32.0 ** -0.5
NEG = -1e30
F32 = jnp.float32
BF16 = jnp.bfloat16
BIG = 24 * 1024 * 1024
SMALL = 12 * 1024 * 1024
VM = pl.BlockSpec(memory_space=pltpu.VMEM)
FAR = pl.BlockSpec(memory_space=pltpu.HBM)


def iota(shape, dim):
    return lax.broadcasted_iota(jnp.int32, shape, dim)


def layer_norm(rows, gain):
    x = rows.astype(F32)
    centred = x - jnp.mean(x, axis=-1, keepdims=True)
    variance = jnp.mean(centred * centred, axis=-1, keepdims=True)
    return (centred * lax.rsqrt(variance + 1e-5) * gain).astype(BF16)


def dot(a, b):
    return jnp.dot(a, b, preferred_element_type=F32)


def dot_t(a, b):
    return lax.dot_general(a, b, (((1,), (1,)), ((), ())), preferred_element_type=F32)


def gelu(z):
    inner = 0.7978845608028654 * (z + 0.044715 * (z * z * z))
    return 0.5 * z * (1.0 + jnp.tanh(inner))


def head_masks(count):
    lane = iota((count, 128), 1) // 32
    return [lane == h for h in range(4)]


def attend_units(units):
    n = units[0][0].shape[0]
    masks = head_masks(n)
    zero = jnp.zeros((n, 128), BF16)
    scores = []
    for q, k, _, bias in units:
        stacked = jnp.concatenate([jnp.where(m, q, zero) for m in masks], axis=0)
        scores.append(dot_t(stacked, k) + bias)
    tops = [jnp.max(s, axis=-1, keepdims=True) for s in scores]
    probs = [jnp.exp2(s - t).astype(BF16) for s, t in zip(scores, tops)]
    outs = []
    for unit, p in zip(units, probs):
        both = dot(p, unit[2])
        top, low = both[:n, :128], both[:n, 128:]
        for h in range(1, 4):
            part = both[h * n : (h + 1) * n]
            top = jnp.where(masks[h], part[:, :128], top)
            low = jnp.where(masks[h], part[:, 128:], low)
        outs.append((top / low).astype(BF16))
    return outs


def finish_rows(attended, stream, gain, wp, wu, wd):
    mixed = (dot(attended, wp[...]) + stream.astype(F32)).astype(BF16)
    normed = layer_norm(mixed, gain)
    acc = mixed.astype(F32)
    for c in range(2):
        hidden = gelu(dot(normed, wu[:, c * 1024 : (c + 1) * 1024])).astype(BF16)
        acc = acc + dot(hidden, wd[c * 1024 : (c + 1) * 1024, :])
    return acc


def query_kernel(x_ref, gains_ref, w_ref, q_ref):
    for half in range(2):
        rows = slice(half * 256, (half + 1) * 256)
        normed = layer_norm(x_ref[rows, :], gains_ref[0:1, :])
        q_ref[rows, :] = (dot(normed, w_ref[0, :, :512]) * QSCALE).astype(BF16)


def query_call(x, gains, wqkv):
    return pl.pallas_call(
        query_kernel,
        in_specs=[VM] * 3,
        out_specs=VM,
        out_shape=pltpu.VMEM((512, 512), BF16),
        compiler_params=pltpu.CompilerParams(vmem_limit_bytes=SMALL),
        cost_estimate=pl.CostEstimate(flops=2 * 512 ** 3, transcendentals=0, bytes_accessed=3 * 512 * 1024),
        name="query",
    )(x, gains, wqkv)


def spread(table, n):
    base = jnp.broadcast_to(table[n : n + 1, :], (16, table.shape[1]))
    return pltpu.roll(base, 0, 1, stride=1, stride_axis=0)


def local_bias_kernel(place_ref, table_ref, bias_ref):
    first_row = place_ref[0]
    first_col = place_ref[1]
    row = iota((64, 256), 0)
    lane = iota((64, 256), 1)
    qi = row // 16
    qj = row % 16
    kr = lane // 24
    kc = lane - kr * 24
    col_q = first_col + qj
    col_a = jnp.clip(col_q - 3, 0, MAP - 7)
    col_k = first_col + kc - 3
    col_ok = (col_k >= col_a) & (col_k <= col_a + 6)
    oks = []
    for block in (0, 1, 7):
        row_q = first_row + 4 * block + qi
        row_a = jnp.clip(row_q - 3, 0, MAP - 7)
        row_k = first_row + 4 * block - 3 + kr
        oks.append(col_ok & (row_k >= row_a) & (row_k <= row_a + 6))
    rolled = [pltpu.roll(table_ref[...], 512 - (24 * (3 - i) + 3), 1) for i in range(4)]
    for n in range(HEADS):
        parts = [spread(rolled[i], n)[:, :256] for i in range(4)]
        full = jnp.concatenate(parts, axis=0)
        at = (n % 4) * 64
        for c in range(3):
            bias_ref[c, n // 4, at : at + 64, :] = jnp.where(oks[c], full, NEG)


def local_bias_call(place, table):
    return pl.pallas_call(
        local_bias_kernel,
        in_specs=[pl.BlockSpec(memory_space=pltpu.SMEM), VM],
        out_specs=VM,
        out_shape=pltpu.VMEM((3, 4, 256, 256), F32),
        compiler_params=pltpu.CompilerParams(vmem_limit_bytes=SMALL),
        cost_estimate=pl.CostEstimate(flops=4_000_000, transcendentals=0, bytes_accessed=3 * 1024 * 1024),
        name="local_bias",
    )(place, table)


def group_bias_kernel(table_ref, bias_ref):
    row = iota((32, 128), 0)
    lane = iota((32, 128), 1)
    qi = row // 16
    qj = row % 16
    kr = lane // 16
    kc = lane % 16
    col_a = jnp.clip(qj - 3, 0, 9)
    col_ok = (kc >= col_a) & (kc <= col_a + 6)
    classes = ((0, 0), (1, 0), (2, 1), (6, 8), (7, 8))
    rolled = [pltpu.roll(table_ref[...], 256 - (step * 16 + 6), 1) for step in range(8)]
    for n in range(HEADS):
        at = (n % 4) * 32
        for c, (block, start) in enumerate(classes):
            parts = [spread(rolled[start - 2 * block - i + 7], n)[:, :128] for i in range(2)]
            row_a = jnp.clip(2 * block + qi - 3, 0, 9)
            row_k = start + kr
            ok = col_ok & (row_k >= row_a) & (row_k <= row_a + 6)
            bias_ref[c, n // 4, at : at + 32, :] = jnp.where(ok, jnp.concatenate(parts, axis=0), NEG)


def group_bias_call(table):
    return pl.pallas_call(
        group_bias_kernel,
        in_specs=[VM],
        out_specs=VM,
        out_shape=pltpu.VMEM((5, 4, 128, 128), F32),
        compiler_params=pltpu.CompilerParams(vmem_limit_bytes=SMALL),
        cost_estimate=pl.CostEstimate(flops=4_000_000, transcendentals=0, bytes_accessed=1_300_000),
        name="group_bias",
    )(table)


def fetch_weights(layer, far, near, sems):
    copies = [pltpu.make_async_copy(a.at[layer], b, sems.at[i]) for i, (a, b) in enumerate(zip(far, near))]
    for c in copies:
        c.start()
    return copies


WEIGHT_SCRATCH = [
    pltpu.VMEM((512, 512), BF16),
    pltpu.VMEM((512, 2048), BF16),
    pltpu.VMEM((2048, 512), BF16),
    pltpu.SemaphoreType.DMA((3,)),
]


def send_rows(done, stage, pieces):
    for at, block, slot in pieces:
        for f in range(4):
            stage[pl.ds(block * 256 + slot * 4 + f, 16, stride=16), :] = done[at : at + 16, f * 128 : (f + 1) * 128]


def put_values(v_s, rows, value):
    for g in range(4):
        v_s[rows, g * 256 : g * 256 + 128] = value[:, g * 128 : (g + 1) * 128]


def block_units(q, k, v, bias):
    return [
        (
            q[:, g * 128 : (g + 1) * 128],
            k[:, g * 128 : (g + 1) * 128],
            v[:, g * 256 : (g + 1) * 256],
            bias[g],
        )
        for g in range(4)
    ]


def inner_kernel(
    wide_ref, q_ref, gains_ref, bias, wqkv, wp_far, wu_far, wd_far,
    a_ref, k_s, v_s, wp, wu, wd, sems,
):
    copies = fetch_weights(0, (wp_far, wu_far, wd_far), (wp, wu, wd), sems)
    v_s[...] = jnp.ones((928, 1024), BF16)
    for r in range(2):
        rows = slice(64 + r * 400, 64 + min((r + 1) * 400, 784))
        normed = layer_norm(wide_ref[r * 400 : min((r + 1) * 400, 784), :], gains_ref[0:1, :])
        k_s[rows, :] = dot(normed, wqkv[0, :, 512:1024]).astype(BF16)
        put_values(v_s, rows, dot(normed, wqkv[0, :, 1024:]).astype(BF16))
    for b in range(1, 7):
        keys = slice(96 * b, 96 * b + 256)
        rows = slice(64 * b, 64 * b + 64)
        outs = attend_units(block_units(q_ref[rows, :], k_s[keys, :], v_s[keys, :], bias[1]))
        for g in range(4):
            a_ref[rows, g * 128 : (g + 1) * 128] = outs[g]
    a_ref[0:64, :] = jnp.zeros((64, 512), BF16)
    a_ref[448:512, :] = jnp.zeros((64, 512), BF16)
    for c in copies:
        c.wait()


def inner_call(wide, q, gains, bias, wqkv, wp, wu, wd):
    return pl.pallas_call(
        inner_kernel,
        in_specs=[VM] * 5 + [FAR] * 3,
        out_specs=[VM] * 6,
        out_shape=[
            pltpu.VMEM((512, 512), BF16),
            pltpu.VMEM((928, 512), BF16),
            pltpu.VMEM((928, 1024), BF16),
            pltpu.VMEM((512, 512), BF16),
            pltpu.VMEM((512, 2048), BF16),
            pltpu.VMEM((2048, 512), BF16),
        ],
        scratch_shapes=[pltpu.SemaphoreType.DMA((3,))],
        compiler_params=pltpu.CompilerParams(vmem_limit_bytes=BIG),
        cost_estimate=pl.CostEstimate(flops=4_000_000_000, transcendentals=2_000_000, bytes_accessed=8_000_000),
        name="inner_blocks",
    )(wide, q, gains, bias, wqkv, wp, wu, wd)


def local_kernel(
    edge_ref, x_ref, q_ref, gains_ref, bias, wqkv, a_ref, k_s, v_s, wp, wu, wd, out_ref, k_e, v_e, stage
):
    normed = layer_norm(edge_ref[...], gains_ref[0:1, :])
    gap = jnp.zeros((8, 512), F32)
    v_e[...] = jnp.ones((512, 1024), BF16)
    for lane, is_key in ((512, True), (1024, False)):
        fresh = dot(normed, wqkv[0, :, lane : lane + 512])
        if is_key:
            own = lambda a, b: k_s[a:b, :]
        else:
            own = lambda a, b: jnp.concatenate([v_s[a:b, g * 256 : g * 256 + 128] for g in range(4)], axis=1)
        above = (jnp.concatenate([fresh[64:72], gap], axis=0) + own(64, 80).astype(F32)).astype(BF16)
        below = (jnp.concatenate([gap, fresh[72:80]], axis=0) + own(832, 848).astype(F32)).astype(BF16)
        pieces = [
            (0, fresh[:64].astype(BF16)),
            (64, above),
            (80, own(80, 256)),
            (256, own(672, 832)),
            (416, below),
            (432, fresh[80:144].astype(BF16)),
            (496, jnp.zeros((16, 512), BF16)),
        ]
        for at, piece in pieces:
            rows = slice(at, at + piece.shape[0])
            if is_key:
                k_e[rows, :] = piece
            else:
                put_values(v_e, rows, piece)
    units = block_units(q_ref[0:64, :], k_e[:256, :], v_e[:256, :], bias[0])
    units += block_units(q_ref[448:512, :], k_e[256:, :], v_e[256:, :], bias[2])
    outs = attend_units(units)
    attended = jnp.concatenate(
        [jnp.concatenate(outs[:4], axis=1), a_ref[64:448, :], jnp.concatenate(outs[4:], axis=1)], axis=0
    )
    done = finish_rows(attended, x_ref[...], gains_ref[1:2, :], wp, wu, wd)
    send_rows(done, stage, [(i * 16, i % 16 // 2, i % 2 * 2 + i // 16) for i in range(32)])
    out_ref[...] = stage[...].reshape(128, 16, 128).astype(BF16)


def local_call(edge, x, q, gains, bias, wqkv, inner):
    return pl.pallas_call(
        local_kernel,
        in_specs=[VM] * 12,
        out_specs=VM,
        out_shape=pltpu.VMEM((128, 16, 128), BF16),
        scratch_shapes=[
            pltpu.VMEM((512, 512), BF16),
            pltpu.VMEM((512, 1024), BF16),
            pltpu.VMEM((2048, 128), F32),
        ],
        compiler_params=pltpu.CompilerParams(vmem_limit_bytes=BIG),
        cost_estimate=pl.CostEstimate(flops=4_000_000_000, transcendentals=2_000_000, bytes_accessed=8_000_000),
        name="local_layer",
    )(edge, x, q, gains, bias, wqkv, *inner)


def group_kernel(
    in_ref, gains_ref, bias, wqkv, wp_far, wu_far, wd_far, out_ref,
    x_s, q_s, k_s, v_s, a_s, stage, wp, wu, wd, sems,
):
    copies = fetch_weights(1, (wp_far, wu_far, wd_far), (wp, wu, wd), sems)
    stage[...] = in_ref[...].astype(F32).reshape(2048, 128)
    for g in range(2):
        for p in range(16):
            r, half = p // 2, p % 2
            at = g * 256 + p * 16
            for f in range(4):
                x_s[at : at + 16, f * 128 : (f + 1) * 128] = stage[
                    pl.ds(r * 256 + (g * 2 + half) * 4 + f, 16, stride=16), :
                ]
    v_s[...] = jnp.ones((512, 1024), BF16)
    for g in range(2):
        rows = slice(g * 256, (g + 1) * 256)
        normed = layer_norm(x_s[rows, :], gains_ref[2:3, :])
        q_s[rows, :] = (dot(normed, wqkv[1, :, :512]) * QSCALE).astype(BF16)
        k_s[rows, :] = dot(normed, wqkv[1, :, 512:1024]).astype(BF16)
        value = dot(normed, wqkv[1, :, 1024:]).astype(BF16)
        for h in range(4):
            v_s[rows, h * 256 : h * 256 + 128] = value[:, h * 128 : (h + 1) * 128]

    def attend(b, carry):
        start = min(max(2 * b - 3, 0), 8)
        kind = b if b < 2 else 2 if b < 6 else b - 3
        units = []
        for g in range(2):
            at_q = g * 256 + b * 32
            at_k = g * 256 + start * 16
            for h in range(4):
                units.append(
                    (
                        q_s[pl.ds(at_q, 32), h * 128 : (h + 1) * 128],
                        k_s[pl.ds(at_k, 128), h * 128 : (h + 1) * 128],
                        v_s[pl.ds(at_k, 128), h * 256 : (h + 1) * 256],
                        bias[kind, h],
                    )
                )
        outs = attend_units(units)
        for g in range(2):
            at_q = g * 256 + b * 32
            for h in range(4):
                a_s[pl.ds(at_q, 32), h * 128 : (h + 1) * 128] = outs[g * 4 + h]
        return carry

    for b in range(8):
        attend(b, 0)
    for c in copies:
        c.wait()
    done = finish_rows(a_s[...], x_s[...], gains_ref[3:4, :], wp, wu, wd)
    send_rows(done, stage, [(i * 16, i % 16 // 2, i // 16 * 2 + i % 2) for i in range(32)])
    out_ref[...] = stage[...].reshape(128, 16, 128).astype(BF16)


def group_call(rows, gains, bias, wqkv, wp, wu, wd):
    return pl.pallas_call(
        group_kernel,
        in_specs=[VM] * 4 + [FAR] * 3,
        out_specs=VM,
        out_shape=pltpu.VMEM((128, 16, 128), BF16),
        scratch_shapes=[
            pltpu.VMEM((512, 512), F32),
            pltpu.VMEM((512, 512), BF16),
            pltpu.VMEM((512, 512), BF16),
            pltpu.VMEM((512, 1024), BF16),
            pltpu.VMEM((512, 512), BF16),
            pltpu.VMEM((2048, 128), F32),
        ]
        + WEIGHT_SCRATCH,
        compiler_params=pltpu.CompilerParams(vmem_limit_bytes=BIG),
        cost_estimate=pl.CostEstimate(flops=7_000_000_000, transcendentals=3_000_000, bytes_accessed=10_000_000),
        name="group_layer",
    )(rows, gains, bias, wqkv, wp, wu, wd)


def place_kernel(in_ref, out_ref, stage):
    stage[...] = in_ref[...].astype(F32).reshape(2048, 128)
    for r in range(8):
        for slot in range(4):
            parts = [stage[pl.ds(r * 256 + slot * 4 + f, 16, stride=16), :] for f in range(4)]
            out_ref[slot % 2 * 16 + 2 * r + slot // 2] = jnp.concatenate(parts, axis=1).astype(BF16)


def place_call(rows):
    return pl.pallas_call(
        place_kernel,
        in_specs=[VM],
        out_specs=VM,
        out_shape=jax.ShapeDtypeStruct((TR, TC, D), BF16),
        scratch_shapes=[pltpu.VMEM((2048, 128), F32)],
        compiler_params=pltpu.CompilerParams(vmem_limit_bytes=SMALL),
        name="place",
    )(rows)


def edges(cells, axis, dim):
    count = lax.axis_size(axis)
    size = cells.shape[dim]
    head = lax.slice_in_dim(cells, 0, 3, axis=dim)
    tail = lax.slice_in_dim(cells, size - 3, size, axis=dim)
    before = lax.ppermute(tail, axis, [(i, (i + 1) % count) for i in range(count)])
    after = lax.ppermute(head, axis, [((i + 1) % count, i) for i in range(count)])
    return before, after


def exchange(rows):
    return lax.all_to_all(rows, ("row", "col"), 0, 0, tiled=True)


def body(tokens, norm_gains, qkv_weight, rel_bias, proj_weight, up_weight, down_weight):
    x = tokens.reshape(TR * TC, D)
    table = rel_bias * LOG2E
    local_table = jnp.pad(table[0], ((0, 0), (0, 0), (0, 11))).reshape(HEADS, 312)
    local_table = jnp.pad(local_table, ((0, 0), (0, 200)))
    group_table = jnp.pad(table[1], ((0, 0), (1, 2), (0, 3))).reshape(HEADS, 256)
    place = jnp.stack([lax.axis_index("row") * TR, lax.axis_index("col") * TC]).astype(jnp.int32)

    near = lambda a: pltpu.with_memory_space_constraint(a, pltpu.VMEM)
    far = lambda a: pltpu.with_memory_space_constraint(a, pltpu.HBM)
    wqkv, wp, wu, wd = near(qkv_weight), far(proj_weight), far(up_weight), far(down_weight)
    x = near(x)
    q = query_call(x, norm_gains, wqkv)
    local_bias = local_bias_call(place, local_table)
    group_bias = group_bias_call(group_table)
    left, right = edges(tokens, "col", 1)
    left, right, q, local_bias, group_bias = lax.optimization_barrier((left, right, q, local_bias, group_bias))
    wide = jnp.concatenate([left, tokens, right, jnp.zeros((TR, 2, D), BF16)], axis=1)
    top, bottom = edges(wide, "row", 0)
    padded = jnp.pad(wide.reshape(TR * 24, D), ((8, 8), (0, 0)))
    edge = jnp.concatenate([top.reshape(72, D), bottom.reshape(72, D)], axis=0)
    inner = inner_call(near(padded), near(q), norm_gains, near(local_bias), wqkv, wp, wu, wd)
    sent = local_call(near(edge), x, near(q), norm_gains, near(local_bias), wqkv, inner)
    got = exchange(sent)
    back = group_call(near(got), norm_gains, near(group_bias), wqkv, wp, wu, wd)
    return place_call(near(exchange(back)))


def solution(mesh):
    placed = (P("row", "col", None), P(), P(), P(), P(), P(), P())
    return jax.shard_map(
        body, mesh=mesh, in_specs=placed, out_specs=P("row", "col", None), check_vma=False
    )
```

```python
import jax
import jax.numpy as jnp
from jax import lax
from jax.experimental import pallas as pl
from jax.experimental.pallas import tpu as pltpu
from jax.sharding import PartitionSpec as P

D = 512
HEADS = 16
FF = 2048
TR = 32
TC = 16
MAP = 256
LOG2E = 1.4426950408889634
QSCALE = LOG2E * 32.0 ** -0.5
NEG = -1e30
F32 = jnp.float32
BF16 = jnp.bfloat16
BIG = 24 * 1024 * 1024
SMALL = 12 * 1024 * 1024
VM = pl.BlockSpec(memory_space=pltpu.VMEM)
FAR = pl.BlockSpec(memory_space=pltpu.HBM)


def iota(shape, dim):
    return lax.broadcasted_iota(jnp.int32, shape, dim)


def layer_norm(rows, gain):
    x = rows.astype(F32)
    centred = x - jnp.mean(x, axis=-1, keepdims=True)
    variance = jnp.mean(centred * centred, axis=-1, keepdims=True)
    return (centred * lax.rsqrt(variance + 1e-5) * gain).astype(BF16)


def dot(a, b):
    return jnp.dot(a, b, preferred_element_type=F32)


def dot_t(a, b):
    return lax.dot_general(a, b, (((1,), (1,)), ((), ())), preferred_element_type=F32)


def gelu(z):
    inner = 0.7978845608028654 * (z + 0.044715 * (z * z * z))
    return 0.5 * z * (1.0 + jnp.tanh(inner))


def head_masks(count):
    lane = iota((count, 128), 1) // 32
    return [lane == h for h in range(4)]


def attend_units(units):
    n = units[0][0].shape[0]
    masks = head_masks(n)
    zero = jnp.zeros((n, 128), BF16)
    scores = []
    for q, k, _, bias in units:
        stacked = jnp.concatenate([jnp.where(m, q, zero) for m in masks], axis=0)
        scores.append(dot_t(stacked, k) + bias)
    tops = [jnp.max(s, axis=-1, keepdims=True) for s in scores]
    probs = [jnp.exp2(s - t).astype(BF16) for s, t in zip(scores, tops)]
    outs = []
    for unit, p in zip(units, probs):
        both = dot(p, unit[2])
        top, low = both[:n, :128], both[:n, 128:]
        for h in range(1, 4):
            part = both[h * n : (h + 1) * n]
            top = jnp.where(masks[h], part[:, :128], top)
            low = jnp.where(masks[h], part[:, 128:], low)
        outs.append((top / low).astype(BF16))
    return outs


def finish_rows(attended, stream, gain, wp, wu, wd):
    mixed = (dot(attended, wp[...]) + stream.astype(F32)).astype(BF16)
    normed = layer_norm(mixed, gain)
    acc = mixed.astype(F32)
    for c in range(2):
        hidden = gelu(dot(normed, wu[:, c * 1024 : (c + 1) * 1024])).astype(BF16)
        acc = acc + dot(hidden, wd[c * 1024 : (c + 1) * 1024, :])
    return acc


def query_kernel(x_ref, gains_ref, w_ref, q_ref):
    for half in range(2):
        rows = slice(half * 256, (half + 1) * 256)
        normed = layer_norm(x_ref[rows, :], gains_ref[0:1, :])
        q_ref[rows, :] = (dot(normed, w_ref[:, :512]) * QSCALE).astype(BF16)


def query_call(x, gains, wqkv):
    return pl.pallas_call(
        query_kernel,
        in_specs=[VM] * 3,
        out_specs=VM,
        out_shape=pltpu.VMEM((512, 512), BF16),
        compiler_params=pltpu.CompilerParams(vmem_limit_bytes=SMALL),
        cost_estimate=pl.CostEstimate(flops=2 * 512 ** 3, transcendentals=0, bytes_accessed=3 * 512 * 1024),
        name="query",
    )(x, gains, wqkv)


def spread(table, n):
    base = jnp.broadcast_to(table[n : n + 1, :], (16, table.shape[1]))
    return pltpu.roll(base, 0, 1, stride=1, stride_axis=0)


def flatten_table(table_ref, pad, layer, width, stride, offset):
    flat = jnp.zeros((HEADS, width), F32)
    rest = jnp.zeros((HEADS, width - 128), F32)
    for y in range(13):
        pad[y, :, 0:13] = table_ref[layer, y] * LOG2E
        row = jnp.concatenate([pad[y], rest], axis=1)
        at = stride * y + offset
        flat = flat + (pltpu.roll(row, at, 1) if at else row)
    return flat


def bias_kernel(place_ref, table_ref, w_far, local_ref, group_ref, w_near, pad, sem):
    fetch = pltpu.make_async_copy(w_far.at[0], w_near, sem)
    fetch.start()
    pad[...] = jnp.zeros((13, HEADS, 128), F32)
    local_bias(place_ref, flatten_table(table_ref, pad, 0, 512, 24, 0), local_ref)
    group_bias(flatten_table(table_ref, pad, 1, 256, 16, 16), group_ref)
    fetch.wait()


def local_bias(place_ref, flat, bias_ref):
    first_row = place_ref[0]
    first_col = place_ref[1]
    row = iota((64, 256), 0)
    lane = iota((64, 256), 1)
    qi = row // 16
    qj = row % 16
    kr = lane // 24
    kc = lane - kr * 24
    col_q = first_col + qj
    col_a = jnp.clip(col_q - 3, 0, MAP - 7)
    col_k = first_col + kc - 3
    col_ok = (col_k >= col_a) & (col_k <= col_a + 6)
    oks = []
    for block in (0, 1, 7):
        row_q = first_row + 4 * block + qi
        row_a = jnp.clip(row_q - 3, 0, MAP - 7)
        row_k = first_row + 4 * block - 3 + kr
        oks.append(col_ok & (row_k >= row_a) & (row_k <= row_a + 6))
    rolled = [pltpu.roll(flat, 512 - (24 * (3 - i) + 3), 1) for i in range(4)]
    for n in range(HEADS):
        parts = [spread(rolled[i], n)[:, :256] for i in range(4)]
        full = jnp.concatenate(parts, axis=0)
        at = (n % 4) * 64
        for c in range(3):
            bias_ref[c, n // 4, at : at + 64, :] = jnp.where(oks[c], full, NEG)


def group_bias(flat, bias_ref):
    row = iota((32, 128), 0)
    lane = iota((32, 128), 1)
    qi = row // 16
    qj = row % 16
    kr = lane // 16
    kc = lane % 16
    col_a = jnp.clip(qj - 3, 0, 9)
    col_ok = (kc >= col_a) & (kc <= col_a + 6)
    classes = ((0, 0), (1, 0), (2, 1), (6, 8), (7, 8))
    rolled = [pltpu.roll(flat, 256 - (step * 16 + 6), 1) for step in range(8)]
    for n in range(HEADS):
        at = (n % 4) * 32
        for c, (block, start) in enumerate(classes):
            parts = [spread(rolled[start - 2 * block - i + 7], n)[:, :128] for i in range(2)]
            row_a = jnp.clip(2 * block + qi - 3, 0, 9)
            row_k = start + kr
            ok = col_ok & (row_k >= row_a) & (row_k <= row_a + 6)
            bias_ref[c, n // 4, at : at + 32, :] = jnp.where(ok, jnp.concatenate(parts, axis=0), NEG)


def bias_call(place, table, wqkv):
    return pl.pallas_call(
        bias_kernel,
        in_specs=[pl.BlockSpec(memory_space=pltpu.SMEM), VM, FAR],
        out_specs=[VM] * 3,
        out_shape=[
            pltpu.VMEM((3, 4, 256, 256), F32),
            pltpu.VMEM((5, 4, 128, 128), F32),
            pltpu.VMEM((512, 1536), BF16),
        ],
        scratch_shapes=[pltpu.VMEM((13, HEADS, 128), F32), pltpu.SemaphoreType.DMA(())],
        compiler_params=pltpu.CompilerParams(vmem_limit_bytes=SMALL),
        cost_estimate=pl.CostEstimate(flops=8_000_000, transcendentals=0, bytes_accessed=5 * 1024 * 1024),
        name="biases",
    )(place, table, wqkv)


def fetch_weights(layer, far, near, sems):
    copies = [pltpu.make_async_copy(a.at[layer], b, sems.at[i]) for i, (a, b) in enumerate(zip(far, near))]
    for c in copies:
        c.start()
    return copies


WEIGHT_SCRATCH = [
    pltpu.VMEM((512, 512), BF16),
    pltpu.VMEM((512, 2048), BF16),
    pltpu.VMEM((2048, 512), BF16),
    pltpu.SemaphoreType.DMA((3,)),
]


def send_rows(done, stage, pieces):
    for at, block, slot in pieces:
        for f in range(4):
            stage[pl.ds(block * 256 + slot * 4 + f, 16, stride=16), :] = done[at : at + 16, f * 128 : (f + 1) * 128]


def put_values(v_s, rows, value):
    for g in range(4):
        v_s[rows, g * 256 : g * 256 + 128] = value[:, g * 128 : (g + 1) * 128]


def block_units(q, k, v, bias):
    return [
        (
            q[:, g * 128 : (g + 1) * 128],
            k[:, g * 128 : (g + 1) * 128],
            v[:, g * 256 : (g + 1) * 256],
            bias[g],
        )
        for g in range(4)
    ]


def inner_kernel(
    wide_ref, q_ref, gains_ref, bias, wqkv, wp_far, wu_far, wd_far,
    a_ref, k_s, v_s, wp, wu, wd, sems,
):
    copies = fetch_weights(0, (wp_far, wu_far, wd_far), (wp, wu, wd), sems)
    v_s[...] = jnp.ones((928, 1024), BF16)
    for r in range(2):
        rows = slice(64 + r * 400, 64 + min((r + 1) * 400, 784))
        normed = layer_norm(wide_ref[r * 400 : min((r + 1) * 400, 784), :], gains_ref[0:1, :])
        k_s[rows, :] = dot(normed, wqkv[:, 512:1024]).astype(BF16)
        put_values(v_s, rows, dot(normed, wqkv[:, 1024:]).astype(BF16))
    for b in range(1, 7):
        keys = slice(96 * b, 96 * b + 256)
        rows = slice(64 * b, 64 * b + 64)
        outs = attend_units(block_units(q_ref[rows, :], k_s[keys, :], v_s[keys, :], bias[1]))
        for g in range(4):
            a_ref[rows, g * 128 : (g + 1) * 128] = outs[g]
    a_ref[0:64, :] = jnp.zeros((64, 512), BF16)
    a_ref[448:512, :] = jnp.zeros((64, 512), BF16)
    for c in copies:
        c.wait()


def inner_call(wide, q, gains, bias, wqkv, wp, wu, wd):
    return pl.pallas_call(
        inner_kernel,
        in_specs=[VM] * 5 + [FAR] * 3,
        out_specs=[VM] * 6,
        out_shape=[
            pltpu.VMEM((512, 512), BF16),
            pltpu.VMEM((928, 512), BF16),
            pltpu.VMEM((928, 1024), BF16),
            pltpu.VMEM((512, 512), BF16),
            pltpu.VMEM((512, 2048), BF16),
            pltpu.VMEM((2048, 512), BF16),
        ],
        scratch_shapes=[pltpu.SemaphoreType.DMA((3,))],
        compiler_params=pltpu.CompilerParams(vmem_limit_bytes=BIG),
        cost_estimate=pl.CostEstimate(flops=4_000_000_000, transcendentals=2_000_000, bytes_accessed=8_000_000),
        name="inner_blocks",
    )(wide, q, gains, bias, wqkv, wp, wu, wd)


def local_kernel(
    edge_ref, x_ref, q_ref, gains_ref, bias, wqkv, w_far, a_ref, k_s, v_s, wp, wu, wd, out_ref, w_next,
    k_e, v_e, stage, sem,
):
    fetch = pltpu.make_async_copy(w_far.at[1], w_next, sem)
    fetch.start()
    normed = layer_norm(edge_ref[...], gains_ref[0:1, :])
    gap = jnp.zeros((8, 512), F32)
    v_e[...] = jnp.ones((512, 1024), BF16)
    for lane, is_key in ((512, True), (1024, False)):
        fresh = dot(normed, wqkv[:, lane : lane + 512])
        if is_key:
            own = lambda a, b: k_s[a:b, :]
        else:
            own = lambda a, b: jnp.concatenate([v_s[a:b, g * 256 : g * 256 + 128] for g in range(4)], axis=1)
        above = (jnp.concatenate([fresh[64:72], gap], axis=0) + own(64, 80).astype(F32)).astype(BF16)
        below = (jnp.concatenate([gap, fresh[72:80]], axis=0) + own(832, 848).astype(F32)).astype(BF16)
        pieces = [
            (0, fresh[:64].astype(BF16)),
            (64, above),
            (80, own(80, 256)),
            (256, own(672, 832)),
            (416, below),
            (432, fresh[80:144].astype(BF16)),
            (496, jnp.zeros((16, 512), BF16)),
        ]
        for at, piece in pieces:
            rows = slice(at, at + piece.shape[0])
            if is_key:
                k_e[rows, :] = piece
            else:
                put_values(v_e, rows, piece)
    units = block_units(q_ref[0:64, :], k_e[:256, :], v_e[:256, :], bias[0])
    units += block_units(q_ref[448:512, :], k_e[256:, :], v_e[256:, :], bias[2])
    outs = attend_units(units)
    attended = jnp.concatenate(
        [jnp.concatenate(outs[:4], axis=1), a_ref[64:448, :], jnp.concatenate(outs[4:], axis=1)], axis=0
    )
    done = finish_rows(attended, x_ref[...], gains_ref[1:2, :], wp, wu, wd)
    send_rows(done, stage, [(i * 16, i % 16 // 2, i % 2 * 2 + i // 16) for i in range(32)])
    out_ref[...] = stage[...].reshape(128, 16, 128).astype(BF16)
    fetch.wait()


def local_call(edge, x, q, gains, bias, wqkv, w_far, inner):
    return pl.pallas_call(
        local_kernel,
        in_specs=[VM] * 6 + [FAR] + [VM] * 6,
        out_specs=[VM, VM],
        out_shape=[pltpu.VMEM((128, 16, 128), BF16), pltpu.VMEM((512, 1536), BF16)],
        scratch_shapes=[
            pltpu.VMEM((512, 512), BF16),
            pltpu.VMEM((512, 1024), BF16),
            pltpu.VMEM((2048, 128), F32),
            pltpu.SemaphoreType.DMA(()),
        ],
        compiler_params=pltpu.CompilerParams(vmem_limit_bytes=BIG),
        cost_estimate=pl.CostEstimate(flops=4_000_000_000, transcendentals=2_000_000, bytes_accessed=8_000_000),
        name="local_layer",
    )(edge, x, q, gains, bias, wqkv, w_far, *inner)


def group_kernel(
    in_ref, gains_ref, bias, wqkv, wp_far, wu_far, wd_far, out_ref,
    x_s, q_s, k_s, v_s, a_s, stage, wp, wu, wd, sems,
):
    copies = fetch_weights(1, (wp_far, wu_far, wd_far), (wp, wu, wd), sems)
    stage[...] = in_ref[...].astype(F32).reshape(2048, 128)
    for g in range(2):
        for p in range(16):
            r, half = p // 2, p % 2
            at = g * 256 + p * 16
            for f in range(4):
                x_s[at : at + 16, f * 128 : (f + 1) * 128] = stage[
                    pl.ds(r * 256 + (g * 2 + half) * 4 + f, 16, stride=16), :
                ]
    v_s[...] = jnp.ones((512, 1024), BF16)
    for g in range(2):
        rows = slice(g * 256, (g + 1) * 256)
        normed = layer_norm(x_s[rows, :], gains_ref[2:3, :])
        q_s[rows, :] = (dot(normed, wqkv[:, :512]) * QSCALE).astype(BF16)
        k_s[rows, :] = dot(normed, wqkv[:, 512:1024]).astype(BF16)
        value = dot(normed, wqkv[:, 1024:]).astype(BF16)
        for h in range(4):
            v_s[rows, h * 256 : h * 256 + 128] = value[:, h * 128 : (h + 1) * 128]

    for b0 in range(0, 8, 2):
        for gs in ((0, 1),):
            units, places = [], []
            for b in range(b0, b0 + 2):
                start = min(max(2 * b - 3, 0), 8)
                kind = b if b < 2 else 2 if b < 6 else b - 3
                for g in gs:
                    at_q = g * 256 + b * 32
                    at_k = g * 256 + start * 16
                    for h in range(4):
                        units.append(
                            (
                                q_s[at_q : at_q + 32, h * 128 : (h + 1) * 128],
                                k_s[at_k : at_k + 128, h * 128 : (h + 1) * 128],
                                v_s[at_k : at_k + 128, h * 256 : (h + 1) * 256],
                                bias[kind, h],
                            )
                        )
                        places.append((at_q, h))
            for (at_q, h), out in zip(places, attend_units(units)):
                a_s[at_q : at_q + 32, h * 128 : (h + 1) * 128] = out
    for c in copies:
        c.wait()
    done = finish_rows(a_s[...], x_s[...], gains_ref[3:4, :], wp, wu, wd)
    send_rows(done, stage, [(i * 16, i % 16 // 2, i // 16 * 2 + i % 2) for i in range(32)])
    out_ref[...] = stage[...].reshape(128, 16, 128).astype(BF16)


def group_call(rows, gains, bias, wqkv, wp, wu, wd):
    return pl.pallas_call(
        group_kernel,
        in_specs=[VM] * 4 + [FAR] * 3,
        out_specs=VM,
        out_shape=pltpu.VMEM((128, 16, 128), BF16),
        scratch_shapes=[
            pltpu.VMEM((512, 512), F32),
            pltpu.VMEM((512, 512), BF16),
            pltpu.VMEM((512, 512), BF16),
            pltpu.VMEM((512, 1024), BF16),
            pltpu.VMEM((512, 512), BF16),
            pltpu.VMEM((2048, 128), F32),
        ]
        + WEIGHT_SCRATCH,
        compiler_params=pltpu.CompilerParams(vmem_limit_bytes=BIG),
        cost_estimate=pl.CostEstimate(flops=7_000_000_000, transcendentals=3_000_000, bytes_accessed=10_000_000),
        name="group_layer",
    )(rows, gains, bias, wqkv, wp, wu, wd)


def place_kernel(in_ref, out_ref, stage):
    stage[...] = in_ref[...].astype(F32).reshape(2048, 128)
    for r in range(8):
        for slot in range(4):
            parts = [stage[pl.ds(r * 256 + slot * 4 + f, 16, stride=16), :] for f in range(4)]
            out_ref[slot % 2 * 16 + 2 * r + slot // 2] = jnp.concatenate(parts, axis=1).astype(BF16)


def place_call(rows):
    return pl.pallas_call(
        place_kernel,
        in_specs=[VM],
        out_specs=VM,
        out_shape=jax.ShapeDtypeStruct((TR, TC, D), BF16),
        scratch_shapes=[pltpu.VMEM((2048, 128), F32)],
        compiler_params=pltpu.CompilerParams(vmem_limit_bytes=SMALL),
        name="place",
    )(rows)


def edges(cells, axis, dim):
    count = lax.axis_size(axis)
    size = cells.shape[dim]
    head = lax.slice_in_dim(cells, 0, 3, axis=dim)
    tail = lax.slice_in_dim(cells, size - 3, size, axis=dim)
    before = lax.ppermute(tail, axis, [(i, (i + 1) % count) for i in range(count)])
    after = lax.ppermute(head, axis, [((i + 1) % count, i) for i in range(count)])
    return before, after


def exchange(rows):
    return lax.all_to_all(rows, ("row", "col"), 0, 0, tiled=True)


def body(tokens, norm_gains, qkv_weight, rel_bias, proj_weight, up_weight, down_weight):
    x = tokens.reshape(TR * TC, D)
    place = jnp.stack([lax.axis_index("row") * TR, lax.axis_index("col") * TC]).astype(jnp.int32)

    near = lambda a: pltpu.with_memory_space_constraint(a, pltpu.VMEM)
    far = lambda a: pltpu.with_memory_space_constraint(a, pltpu.HBM)
    w_far, wp, wu, wd = far(qkv_weight), far(proj_weight), far(up_weight), far(down_weight)
    x = near(x)
    local_bias, group_bias, wqkv = bias_call(place, near(rel_bias.transpose(0, 2, 1, 3)), w_far)
    q = query_call(x, norm_gains, near(wqkv))
    left, right = edges(tokens, "col", 1)
    left, right, q, local_bias, group_bias = lax.optimization_barrier((left, right, q, local_bias, group_bias))
    wqkv, local_bias = near(wqkv), near(local_bias)
    wide = jnp.concatenate([left, tokens, right, jnp.zeros((TR, 2, D), BF16)], axis=1)
    top, bottom = edges(wide, "row", 0)
    padded = jnp.pad(wide.reshape(TR * 24, D), ((8, 8), (0, 0)))
    edge = jnp.concatenate([top.reshape(72, D), bottom.reshape(72, D)], axis=0)
    inner = inner_call(near(padded), near(q), norm_gains, local_bias, wqkv, wp, wu, wd)
    sent, wqkv_next = local_call(near(edge), x, near(q), norm_gains, local_bias, wqkv, w_far, inner)
    got = exchange(sent)
    back = group_call(near(got), norm_gains, near(group_bias), near(wqkv_next), wp, wu, wd)
    return place_call(near(exchange(back)))


def solution(mesh):
    placed = (P("row", "col", None), P(), P(), P(), P(), P(), P())
    return jax.shard_map(
        body, mesh=mesh, in_specs=placed, out_specs=P("row", "col", None), check_vma=False
    )
```

```python
import jax
import jax.numpy as jnp
from jax import lax
from jax.experimental import pallas as pl
from jax.experimental.pallas import tpu as pltpu
from jax.sharding import PartitionSpec as P

D = 512
HEADS = 16
FF = 2048
TR = 32
TC = 16
MAP = 256
LOG2E = 1.4426950408889634
QSCALE = LOG2E * 32.0 ** -0.5
NEG = -1e30
F32 = jnp.float32
BF16 = jnp.bfloat16
BIG = 24 * 1024 * 1024
SMALL = 12 * 1024 * 1024
VM = pl.BlockSpec(memory_space=pltpu.VMEM)
FAR = pl.BlockSpec(memory_space=pltpu.HBM)


def iota(shape, dim):
    return lax.broadcasted_iota(jnp.int32, shape, dim)


def layer_norm(rows, gain):
    x = rows.astype(F32)
    centred = x - jnp.mean(x, axis=-1, keepdims=True)
    variance = jnp.mean(centred * centred, axis=-1, keepdims=True)
    return (centred * lax.rsqrt(variance + 1e-5) * gain).astype(BF16)


def dot(a, b):
    return jnp.dot(a, b, preferred_element_type=F32)


def dot_t(a, b):
    return lax.dot_general(a, b, (((1,), (1,)), ((), ())), preferred_element_type=F32)


def gelu(z):
    inner = 0.7978845608028654 * (z + 0.044715 * (z * z * z))
    return 0.5 * z * (1.0 + jnp.tanh(inner))


def head_masks(count):
    lane = iota((count, 128), 1) // 32
    return [lane == h for h in range(4)]


def attend_units(units):
    n = units[0][0].shape[0]
    masks = head_masks(n)
    zero = jnp.zeros((n, 128), BF16)
    scores = []
    for q, k, _, bias in units:
        stacked = jnp.concatenate([jnp.where(m, q, zero) for m in masks], axis=0)
        scores.append(dot_t(stacked, k) + bias)
    tops = [jnp.max(s, axis=-1, keepdims=True) for s in scores]
    probs = [jnp.exp2(s - t).astype(BF16) for s, t in zip(scores, tops)]
    outs = []
    for unit, p in zip(units, probs):
        both = dot(p, unit[2])
        top, low = both[:n, :128], both[:n, 128:]
        for h in range(1, 4):
            part = both[h * n : (h + 1) * n]
            top = jnp.where(masks[h], part[:, :128], top)
            low = jnp.where(masks[h], part[:, 128:], low)
        outs.append((top / low).astype(BF16))
    return outs


def finish_rows(attended, stream, gain, wp, wu, wd):
    mixed = (dot(attended, wp[...]) + stream.astype(F32)).astype(BF16)
    normed = layer_norm(mixed, gain)
    acc = mixed.astype(F32)
    for c in range(2):
        hidden = gelu(dot(normed, wu[:, c * 1024 : (c + 1) * 1024])).astype(BF16)
        acc = acc + dot(hidden, wd[c * 1024 : (c + 1) * 1024, :])
    return acc


def query_kernel(x_ref, gains_ref, w_ref, q_ref):
    for half in range(2):
        rows = slice(half * 256, (half + 1) * 256)
        normed = layer_norm(x_ref[rows, :], gains_ref[0:1, :])
        q_ref[rows, :] = (dot(normed, w_ref[:, :512]) * QSCALE).astype(BF16)


def query_call(x, gains, wqkv):
    return pl.pallas_call(
        query_kernel,
        in_specs=[VM] * 3,
        out_specs=VM,
        out_shape=pltpu.VMEM((512, 512), BF16),
        compiler_params=pltpu.CompilerParams(vmem_limit_bytes=SMALL),
        cost_estimate=pl.CostEstimate(flops=2 * 512 ** 3, transcendentals=0, bytes_accessed=3 * 512 * 1024),
        name="query",
    )(x, gains, wqkv)


def spread(table, n):
    base = jnp.broadcast_to(table[n : n + 1, :], (16, table.shape[1]))
    return pltpu.roll(base, 0, 1, stride=1, stride_axis=0)


def flatten_table(table_ref, pad, layer, width, stride, offset):
    flat = jnp.zeros((HEADS, width), F32)
    rest = jnp.zeros((HEADS, width - 128), F32)
    for y in range(13):
        pad[y, :, 0:13] = table_ref[layer, y] * LOG2E
        row = jnp.concatenate([pad[y], rest], axis=1)
        at = stride * y + offset
        flat = flat + (pltpu.roll(row, at, 1) if at else row)
    return flat


def bias_kernel(place_ref, table_ref, w_far, local_ref, group_ref, w_near, pad, sem):
    fetch = pltpu.make_async_copy(w_far.at[0], w_near, sem)
    fetch.start()
    pad[...] = jnp.zeros((13, HEADS, 128), F32)
    local_bias(place_ref, flatten_table(table_ref, pad, 0, 512, 24, 0), local_ref)
    group_bias(flatten_table(table_ref, pad, 1, 256, 16, 16), group_ref)
    fetch.wait()


def local_bias(place_ref, flat, bias_ref):
    first_row = place_ref[0]
    first_col = place_ref[1]
    row = iota((64, 256), 0)
    lane = iota((64, 256), 1)
    qi = row // 16
    qj = row % 16
    kr = lane // 24
    kc = lane - kr * 24
    col_q = first_col + qj
    col_a = jnp.clip(col_q - 3, 0, MAP - 7)
    col_k = first_col + kc - 3
    col_ok = (col_k >= col_a) & (col_k <= col_a + 6)
    oks = []
    for block in (0, 1, 7):
        row_q = first_row + 4 * block + qi
        row_a = jnp.clip(row_q - 3, 0, MAP - 7)
        row_k = first_row + 4 * block - 3 + kr
        oks.append(col_ok & (row_k >= row_a) & (row_k <= row_a + 6))
    rolled = [pltpu.roll(flat, 512 - (24 * (3 - i) + 3), 1) for i in range(4)]
    for n in range(HEADS):
        parts = [spread(rolled[i], n)[:, :256] for i in range(4)]
        full = jnp.concatenate(parts, axis=0)
        at = (n % 4) * 64
        for c in range(3):
            bias_ref[c, n // 4, at : at + 64, :] = jnp.where(oks[c], full, NEG)


def group_bias(flat, bias_ref):
    row = iota((32, 128), 0)
    lane = iota((32, 128), 1)
    qi = row // 16
    qj = row % 16
    kr = lane // 16
    kc = lane % 16
    col_a = jnp.clip(qj - 3, 0, 9)
    col_ok = (kc >= col_a) & (kc <= col_a + 6)
    classes = ((0, 0), (1, 0), (2, 1), (6, 8), (7, 8))
    rolled = [pltpu.roll(flat, 256 - (step * 16 + 6), 1) for step in range(8)]
    for n in range(HEADS):
        at = (n % 4) * 32
        for c, (block, start) in enumerate(classes):
            parts = [spread(rolled[start - 2 * block - i + 7], n)[:, :128] for i in range(2)]
            row_a = jnp.clip(2 * block + qi - 3, 0, 9)
            row_k = start + kr
            ok = col_ok & (row_k >= row_a) & (row_k <= row_a + 6)
            bias_ref[c, n // 4, at : at + 32, :] = jnp.where(ok, jnp.concatenate(parts, axis=0), NEG)


def bias_call(place, table, wqkv):
    return pl.pallas_call(
        bias_kernel,
        in_specs=[pl.BlockSpec(memory_space=pltpu.SMEM), VM, FAR],
        out_specs=[VM] * 3,
        out_shape=[
            pltpu.VMEM((3, 4, 256, 256), F32),
            pltpu.VMEM((5, 4, 128, 128), F32),
            pltpu.VMEM((512, 1536), BF16),
        ],
        scratch_shapes=[pltpu.VMEM((13, HEADS, 128), F32), pltpu.SemaphoreType.DMA(())],
        compiler_params=pltpu.CompilerParams(vmem_limit_bytes=SMALL),
        cost_estimate=pl.CostEstimate(flops=8_000_000, transcendentals=0, bytes_accessed=5 * 1024 * 1024),
        name="biases",
    )(place, table, wqkv)


def fetch_weights(layer, far, near, sems):
    copies = [pltpu.make_async_copy(a.at[layer], b, sems.at[i]) for i, (a, b) in enumerate(zip(far, near))]
    for c in copies:
        c.start()
    return copies


WEIGHT_SCRATCH = [
    pltpu.VMEM((512, 512), BF16),
    pltpu.VMEM((512, 2048), BF16),
    pltpu.VMEM((2048, 512), BF16),
    pltpu.SemaphoreType.DMA((3,)),
]


def send_rows(done, stage, pieces):
    for at, block, slot in pieces:
        for f in range(4):
            stage[pl.ds(block * 256 + slot * 4 + f, 16, stride=16), :] = done[at : at + 16, f * 128 : (f + 1) * 128]


def put_values(v_s, rows, value):
    for g in range(4):
        v_s[rows, g * 256 : g * 256 + 128] = value[:, g * 128 : (g + 1) * 128]


def block_units(q, k, v, bias):
    return [
        (
            q[:, g * 128 : (g + 1) * 128],
            k[:, g * 128 : (g + 1) * 128],
            v[:, g * 256 : (g + 1) * 256],
            bias[g],
        )
        for g in range(4)
    ]


def inner_kernel(
    wide_ref, q_ref, gains_ref, bias, wqkv, wp_far, wu_far, wd_far,
    a_ref, k_s, v_s, wp, wu, wd, sems,
):
    copies = fetch_weights(0, (wp_far, wu_far, wd_far), (wp, wu, wd), sems)
    v_s[...] = jnp.ones((928, 1024), BF16)
    for r in range(2):
        rows = slice(64 + r * 400, 64 + min((r + 1) * 400, 784))
        normed = layer_norm(wide_ref[r * 400 : min((r + 1) * 400, 784), :], gains_ref[0:1, :])
        k_s[rows, :] = dot(normed, wqkv[:, 512:1024]).astype(BF16)
        put_values(v_s, rows, dot(normed, wqkv[:, 1024:]).astype(BF16))
    for b in range(1, 7):
        keys = slice(96 * b, 96 * b + 256)
        rows = slice(64 * b, 64 * b + 64)
        outs = attend_units(block_units(q_ref[rows, :], k_s[keys, :], v_s[keys, :], bias[1]))
        for g in range(4):
            a_ref[rows, g * 128 : (g + 1) * 128] = outs[g]
    a_ref[0:64, :] = jnp.zeros((64, 512), BF16)
    a_ref[448:512, :] = jnp.zeros((64, 512), BF16)
    for c in copies:
        c.wait()


def inner_call(wide, q, gains, bias, wqkv, wp, wu, wd):
    return pl.pallas_call(
        inner_kernel,
        in_specs=[VM] * 5 + [FAR] * 3,
        out_specs=[VM] * 6,
        out_shape=[
            pltpu.VMEM((512, 512), BF16),
            pltpu.VMEM((928, 512), BF16),
            pltpu.VMEM((928, 1024), BF16),
            pltpu.VMEM((512, 512), BF16),
            pltpu.VMEM((512, 2048), BF16),
            pltpu.VMEM((2048, 512), BF16),
        ],
        scratch_shapes=[pltpu.SemaphoreType.DMA((3,))],
        compiler_params=pltpu.CompilerParams(vmem_limit_bytes=BIG),
        cost_estimate=pl.CostEstimate(flops=4_000_000_000, transcendentals=2_000_000, bytes_accessed=8_000_000),
        name="inner_blocks",
    )(wide, q, gains, bias, wqkv, wp, wu, wd)


def local_kernel(
    edge_ref, x_ref, q_ref, gains_ref, bias, wqkv, w_far, a_ref, k_s, v_s, wp, wu, wd, out_ref, w_next,
    k_e, v_e, stage, sem,
):
    fetch = pltpu.make_async_copy(w_far.at[1], w_next, sem)
    fetch.start()
    normed = layer_norm(edge_ref[...], gains_ref[0:1, :])
    gap = jnp.zeros((8, 512), F32)
    v_e[...] = jnp.ones((512, 1024), BF16)
    for lane, is_key in ((512, True), (1024, False)):
        fresh = dot(normed, wqkv[:, lane : lane + 512])
        if is_key:
            own = lambda a, b: k_s[a:b, :]
        else:
            own = lambda a, b: jnp.concatenate([v_s[a:b, g * 256 : g * 256 + 128] for g in range(4)], axis=1)
        above = (jnp.concatenate([fresh[64:72], gap], axis=0) + own(64, 80).astype(F32)).astype(BF16)
        below = (jnp.concatenate([gap, fresh[72:80]], axis=0) + own(832, 848).astype(F32)).astype(BF16)
        pieces = [
            (0, fresh[:64].astype(BF16)),
            (64, above),
            (80, own(80, 256)),
            (256, own(672, 832)),
            (416, below),
            (432, fresh[80:144].astype(BF16)),
            (496, jnp.zeros((16, 512), BF16)),
        ]
        for at, piece in pieces:
            rows = slice(at, at + piece.shape[0])
            if is_key:
                k_e[rows, :] = piece
            else:
                put_values(v_e, rows, piece)
    units = block_units(q_ref[0:64, :], k_e[:256, :], v_e[:256, :], bias[0])
    units += block_units(q_ref[448:512, :], k_e[256:, :], v_e[256:, :], bias[2])
    outs = attend_units(units)
    attended = jnp.concatenate(
        [jnp.concatenate(outs[:4], axis=1), a_ref[64:448, :], jnp.concatenate(outs[4:], axis=1)], axis=0
    )
    done = finish_rows(attended, x_ref[...], gains_ref[1:2, :], wp, wu, wd)
    send_rows(done, stage, [(i * 16, i % 16 // 2, i % 2 * 2 + i // 16) for i in range(32)])
    out_ref[...] = stage[...].reshape(128, 16, 128).astype(BF16)
    fetch.wait()


def local_call(edge, x, q, gains, bias, wqkv, w_far, inner):
    return pl.pallas_call(
        local_kernel,
        in_specs=[VM] * 6 + [FAR] + [VM] * 6,
        out_specs=[VM, VM],
        out_shape=[pltpu.VMEM((128, 16, 128), BF16), pltpu.VMEM((512, 1536), BF16)],
        scratch_shapes=[
            pltpu.VMEM((512, 512), BF16),
            pltpu.VMEM((512, 1024), BF16),
            pltpu.VMEM((2048, 128), F32),
            pltpu.SemaphoreType.DMA(()),
        ],
        compiler_params=pltpu.CompilerParams(vmem_limit_bytes=BIG),
        cost_estimate=pl.CostEstimate(flops=4_000_000_000, transcendentals=2_000_000, bytes_accessed=8_000_000),
        name="local_layer",
    )(edge, x, q, gains, bias, wqkv, w_far, *inner)


def group_kernel(
    in_ref, gains_ref, bias, wqkv, wp_far, wu_far, wd_far, out_ref,
    x_s, q_s, k_s, v_s, a_s, stage, wp, wu, wd, sems,
):
    copies = fetch_weights(1, (wp_far, wu_far, wd_far), (wp, wu, wd), sems)
    stage[...] = in_ref[...].astype(F32).reshape(2048, 128)
    for g in range(2):
        for p in range(16):
            r, half = p // 2, p % 2
            at = g * 256 + p * 16
            for f in range(4):
                x_s[at : at + 16, f * 128 : (f + 1) * 128] = stage[
                    pl.ds(r * 256 + (g * 2 + half) * 4 + f, 16, stride=16), :
                ]
    v_s[...] = jnp.ones((512, 1024), BF16)
    for g in range(2):
        rows = slice(g * 256, (g + 1) * 256)
        normed = layer_norm(x_s[rows, :], gains_ref[2:3, :])
        q_s[rows, :] = (dot(normed, wqkv[:, :512]) * QSCALE).astype(BF16)
        k_s[rows, :] = dot(normed, wqkv[:, 512:1024]).astype(BF16)
        value = dot(normed, wqkv[:, 1024:]).astype(BF16)
        for h in range(4):
            v_s[rows, h * 256 : h * 256 + 128] = value[:, h * 128 : (h + 1) * 128]

    for b0 in range(0, 8, 2):
        for gs in ((0, 1),):
            units, places = [], []
            for b in range(b0, b0 + 2):
                start = min(max(2 * b - 3, 0), 8)
                kind = b if b < 2 else 2 if b < 6 else b - 3
                for g in gs:
                    at_q = g * 256 + b * 32
                    at_k = g * 256 + start * 16
                    for h in range(4):
                        units.append(
                            (
                                q_s[at_q : at_q + 32, h * 128 : (h + 1) * 128],
                                k_s[at_k : at_k + 128, h * 128 : (h + 1) * 128],
                                v_s[at_k : at_k + 128, h * 256 : (h + 1) * 256],
                                bias[kind, h],
                            )
                        )
                        places.append((at_q, h))
            for (at_q, h), out in zip(places, attend_units(units)):
                a_s[at_q : at_q + 32, h * 128 : (h + 1) * 128] = out
    for c in copies:
        c.wait()
    done = finish_rows(a_s[...], x_s[...], gains_ref[3:4, :], wp, wu, wd)
    send_rows(done, stage, [(i * 16, i % 16 // 2, i // 16 * 2 + i % 2) for i in range(32)])
    out_ref[...] = stage[...].reshape(128, 16, 128).astype(BF16)


def group_call(rows, gains, bias, wqkv, wp, wu, wd):
    return pl.pallas_call(
        group_kernel,
        in_specs=[VM] * 4 + [FAR] * 3,
        out_specs=VM,
        out_shape=pltpu.VMEM((128, 16, 128), BF16),
        scratch_shapes=[
            pltpu.VMEM((512, 512), F32),
            pltpu.VMEM((512, 512), BF16),
            pltpu.VMEM((512, 512), BF16),
            pltpu.VMEM((512, 1024), BF16),
            pltpu.VMEM((512, 512), BF16),
            pltpu.VMEM((2048, 128), F32),
        ]
        + WEIGHT_SCRATCH,
        compiler_params=pltpu.CompilerParams(vmem_limit_bytes=BIG),
        cost_estimate=pl.CostEstimate(flops=7_000_000_000, transcendentals=3_000_000, bytes_accessed=10_000_000),
        name="group_layer",
    )(rows, gains, bias, wqkv, wp, wu, wd)


def place_kernel(in_ref, out_far, stage, out, sems):
    copies = []
    for part in range(4):
        rows = slice(part * 512, (part + 1) * 512)
        stage[rows, :] = in_ref[part * 32 : (part + 1) * 32].astype(F32).reshape(512, 128)
        for r in (2 * part, 2 * part + 1):
            for slot in range(4):
                pieces = [stage[pl.ds(r * 256 + slot * 4 + f, 16, stride=16), :] for f in range(4)]
                out[slot % 2 * 16 + 2 * r + slot // 2] = jnp.concatenate(pieces, axis=1).astype(BF16)
        for half in range(2):
            at = pl.ds(half * 16 + part * 4, 4)
            copies.append(pltpu.make_async_copy(out.at[at], out_far.at[at], sems.at[part * 2 + half]))
            copies[-1].start()
    for c in copies:
        c.wait()


def place_call(rows):
    return pl.pallas_call(
        place_kernel,
        in_specs=[VM],
        out_specs=FAR,
        out_shape=jax.ShapeDtypeStruct((TR, TC, D), BF16),
        scratch_shapes=[
            pltpu.VMEM((2048, 128), F32),
            pltpu.VMEM((TR, TC, D), BF16),
            pltpu.SemaphoreType.DMA((8,)),
        ],
        compiler_params=pltpu.CompilerParams(vmem_limit_bytes=SMALL),
        name="place",
    )(rows)


def edges(cells, axis, dim):
    count = lax.axis_size(axis)
    size = cells.shape[dim]
    head = lax.slice_in_dim(cells, 0, 3, axis=dim)
    tail = lax.slice_in_dim(cells, size - 3, size, axis=dim)
    before = lax.ppermute(tail, axis, [(i, (i + 1) % count) for i in range(count)])
    after = lax.ppermute(head, axis, [((i + 1) % count, i) for i in range(count)])
    return before, after


def exchange(rows):
    return lax.all_to_all(rows, ("row", "col"), 0, 0, tiled=True)


def body(tokens, norm_gains, qkv_weight, rel_bias, proj_weight, up_weight, down_weight):
    x = tokens.reshape(TR * TC, D)
    place = jnp.stack([lax.axis_index("row") * TR, lax.axis_index("col") * TC]).astype(jnp.int32)

    near = lambda a: pltpu.with_memory_space_constraint(a, pltpu.VMEM)
    far = lambda a: pltpu.with_memory_space_constraint(a, pltpu.HBM)
    w_far, wp, wu, wd = far(qkv_weight), far(proj_weight), far(up_weight), far(down_weight)
    x = near(x)
    local_bias, group_bias, wqkv = bias_call(place, near(rel_bias.transpose(0, 2, 1, 3)), w_far)
    q = query_call(x, norm_gains, near(wqkv))
    left, right = edges(tokens, "col", 1)
    left, right, q, local_bias, group_bias = lax.optimization_barrier((left, right, q, local_bias, group_bias))
    wqkv, local_bias = near(wqkv), near(local_bias)
    wide = jnp.concatenate([left, tokens, right, jnp.zeros((TR, 2, D), BF16)], axis=1)
    top, bottom = edges(wide, "row", 0)
    padded = jnp.pad(wide.reshape(TR * 24, D), ((8, 8), (0, 0)))
    edge = jnp.concatenate([top.reshape(72, D), bottom.reshape(72, D)], axis=0)
    inner = inner_call(near(padded), near(q), norm_gains, local_bias, wqkv, wp, wu, wd)
    sent, wqkv_next = local_call(near(edge), x, near(q), norm_gains, local_bias, wqkv, w_far, inner)
    got = exchange(sent)
    back = group_call(near(got), norm_gains, near(group_bias), near(wqkv_next), wp, wu, wd)
    return place_call(near(exchange(back)))


def solution(mesh):
    placed = (P("row", "col", None), P(), P(), P(), P(), P(), P())
    return jax.shard_map(
        body, mesh=mesh, in_specs=placed, out_specs=P("row", "col", None), check_vma=False
    )
```
